32 devices in a mesh: dp: 8 (over y, x, core), fsdp: 4 (over z).
Axes of the slice: x: 2, y: 2, z: 4, core: 2. Of those that a mesh axis runs over, the one named last changes fastest.
Arguments:
- acts: bfloat16 [16384, 8192], P(('dp', 'fsdp')), may hold values from -6 to 6
- grad_out: bfloat16 [16384, 1024], P(('dp', 'fsdp')), may hold values from -6 to 6
- codes: int32 [128, 16, 1024], P('fsdp'), may hold values from 0 to 65535
- scale_codes: int32 [128, 1024], P('fsdp'), may hold values from 0 to 255
- col_scale: float32 [1024], replicated, may hold values from 0.03 to 0.3
- down_adapter: bfloat16 [64, 8192], P(None, 'fsdp'), may hold values from -0.1796875 to 0.1796875
- up_adapter: bfloat16 [64, 1024], P(None, 'fsdp'), may hold values from -0.1875 to 0.1875
Outputs:
- input_gradient: bfloat16 [16384, 8192], P(('dp', 'fsdp'))
- grad_down: float32 [64, 8192], P(None, 'fsdp')
- grad_up: float32 [64, 1024], P(None, 'fsdp')
The draws below stay inside these ranges and needn't reach their ends.
All inputs are finite; a program needn't handle non-finite values.
Results may differ from the reference program's by a relative error of at most 0.0059.
Values may be sent and summed in bfloat16 or wider, within the bound.
A program may use at most 128 MiB of HBM per device.

```python
import math
import jax
import jax.numpy as jnp
from jax import lax

D = 8192
O = 1024
R = 64
TOK_DEV = 512
TOKEN_TOTAL = 16384


def touch_ends(array, own_key, smallest, top_value):
    longest = array.shape.index(max(array.shape))
    spots = []
    for shift in (0, 1):
        where = [jax.random.randint(jax.random.fold_in(own_key, axis), (), 0, length) for axis, length in enumerate(array.shape)]
        where[longest] = (where[longest] + shift) % array.shape[longest]
        spots.append(tuple(where))
    return array.at[spots[0]].set(smallest).at[spots[1]].set(top_value)


def strengthened(result, key, source, target, blocks, factor):
    def block_of(dim):
        return (jnp.arange(result.shape[dim]) // (result.shape[dim] // blocks)).reshape((-1,) + (1,) * (result.ndim - 1 - dim))

    first = jax.random.permutation(key, blocks)[block_of(target)]
    far = (block_of(target) + blocks // 2) % blocks
    return jnp.where((block_of(source) == first) | (block_of(source) == far), factor * result, result)


def block_levels(key, shape, cuts, smallest, largest):
    def one(dim, shards_of):
        steps = jax.random.uniform(jax.random.fold_in(jax.random.fold_in(key, 6), dim), (shards_of,), jnp.float32, smallest / len(cuts), largest / len(cuts))
        return jnp.repeat(jnp.exp(steps), shape[dim] // shards_of).reshape((-1,) + (1,) * (len(shape) - dim - 1))

    level = one(*cuts[0])
    for cut in cuts[1:]:
        level = level * one(*cut)
    return level


def bell_draw(stream_key, extent, width, bound, cuts=(), kind=jnp.bfloat16):
    result = width * jax.random.normal(stream_key, extent, jnp.float32)
    if cuts:
        result = result * block_levels(stream_key, extent, cuts, -0.22, 0.18)
    return jnp.clip(result, -bound, bound).astype(kind)


def gaussian_with(stream_key, shape, deviation, limit, pieces, heavy, dtype=jnp.bfloat16):
    drawn = deviation * jax.random.normal(stream_key, shape, jnp.float32)
    if pieces:
        drawn = drawn * block_levels(stream_key, shape, pieces, -0.22, 0.18)
    return jnp.clip(strengthened(drawn, jax.random.fold_in(stream_key, 3), *heavy), -limit, limit).astype(dtype)


def setup_inputs(seed: int = 0) -> dict:
    arg_keys = jax.random.split(jax.random.key(seed), 8)
    acts = gaussian_with(arg_keys[0], (TOKEN_TOTAL, D), 1.0, 6.0, ((0, 32),), (0, 1, 32, 2.75))
    grad_out = gaussian_with(arg_keys[1], (TOKEN_TOTAL, O), 1.0, 6.0, ((0, 32),), (0, 1, 32, 2.75))
    codes = touch_ends(jax.random.randint(arg_keys[2], (D // 64, 16, O), 0, 65536), jax.random.fold_in(arg_keys[2], 1), 0, 65535).astype(jnp.int32)
    scale_codes = touch_ends(jax.random.randint(arg_keys[3], (D // 64, O), 0, 256), jax.random.fold_in(arg_keys[3], 1), 0, 255).astype(jnp.int32)
    col_scale = jnp.clip(jnp.exp(jax.random.uniform(arg_keys[4], (O,), jnp.float32, math.log(0.03), math.log(0.3))), 0.03, 0.3)
    down_adapter = bell_draw(arg_keys[5], (R, D), 0.03, 0.1796875, ((1, 4),))
    up_adapter = bell_draw(arg_keys[6], (R, O), O ** -0.5, 0.1875, ((1, 4),))
    return {"acts": acts, "grad_out": grad_out, "codes": codes, "scale_codes": scale_codes, "col_scale": col_scale, "down_adapter": down_adapter, "up_adapter": up_adapter}


adapter_scale = 0.5
nf4_table = [-1.0, -0.6961928009986877, -0.5250730514526367, -0.39491748809814453, -0.28444138169288635, -0.18477343022823334, -0.09105003625154495, 0.0, 0.07958029955625534, 0.16093020141124725, 0.24611230194568634, 0.33791524171829224, 0.44070982933044434, 0.5626170039176941, 0.7229568362236023, 1.0]


def dequantize(codes, scale_codes, col_scale):
    block_count = codes.shape[0]
    columns = codes.shape[2]
    nibbles = jnp.stack([(codes >> (4 * nibble_pos)) & 15 for nibble_pos in range(4)], axis=2)
    levels = jnp.zeros(nibbles.shape, jnp.float32)
    for position, quantum in enumerate(nf4_table):
        levels = jnp.where(nibbles == position, jnp.float32(quantum), levels)
    absmax = (scale_codes.astype(jnp.float32) + 1.0) / 256.0 * col_scale[None, :]
    weight = levels * absmax[:, None, None, :]
    return weight.reshape(block_count * 64, columns).astype(jnp.bfloat16)


def reference(acts, grad_out, codes, scale_codes, col_scale, down_adapter, up_adapter):
    weight = dequantize(codes, scale_codes, col_scale)
    blocks_in = acts.reshape(TOKEN_TOTAL // TOK_DEV, TOK_DEV, D)
    blocks_out = grad_out.reshape(TOKEN_TOTAL // TOK_DEV, TOK_DEV, O)
    scale_factor = adapter_scale * TOKEN_TOTAL ** -0.5

    def one_block(carry, pair):
        act_rows, grad_rows = pair
        mixed = jnp.dot(grad_rows, up_adapter.T, preferred_element_type=jnp.float32).astype(jnp.bfloat16)
        lowered = jnp.dot(act_rows, down_adapter.T, preferred_element_type=jnp.float32).astype(jnp.bfloat16)
        frozen_base = lax.dot_general(grad_rows, weight, (((1,), (1,)), ((), ())), preferred_element_type=jnp.float32)
        operand_side = jnp.dot(mixed, down_adapter, preferred_element_type=jnp.float32)
        incoming_gradient_rows = (frozen_base + adapter_scale * operand_side).astype(jnp.bfloat16)
        term_down = lax.dot_general(mixed, act_rows, (((0,), (0,)), ((), ())), preferred_element_type=jnp.float32)
        term_up = lax.dot_general(lowered, grad_rows, (((0,), (0,)), ((), ())), preferred_element_type=jnp.float32)
        return (carry[0] + term_down, carry[1] + term_up), incoming_gradient_rows

    start = (jnp.zeros((R, D), jnp.float32), jnp.zeros((R, O), jnp.float32))
    totals, grad_blocks = lax.scan(one_block, start, (blocks_in, blocks_out))
    input_gradient = grad_blocks.reshape(TOKEN_TOTAL, D)
    return input_gradient, scale_factor * totals[0], scale_factor * totals[1]
```

```python
import functools

import jax
import jax.numpy as jnp
from jax import lax
from jax.experimental import pallas as pl
from jax.experimental.pallas import tpu as pltpu
from jax.sharding import PartitionSpec as P

MESH = pl.DeviceIdType.MESH
NT = (((1,), (1,)), ((), ()))
adapter_scale = 0.5
nf4_table = [
    -1.0,
    -0.6961928009986877,
    -0.5250730514526367,
    -0.39491748809814453,
    -0.28444138169288635,
    -0.18477343022823334,
    -0.09105003625154495,
    0.0,
    0.07958029955625534,
    0.16093020141124725,
    0.24611230194568634,
    0.33791524171829224,
    0.44070982933044434,
    0.5626170039176941,
    0.7229568362236023,
    1.0,
]
GROUP = 8
LAG1 = 2
LAG2 = 4
AHEAD = 2


def levels_of(words, nibble):
    rows = [jnp.float32(v) for v in nf4_table]
    for bit in range(4):
        on = (words & (1 << (4 * nibble + bit))) != 0
        rows = [jnp.where(on, rows[2 * i + 1], rows[2 * i]) for i in range(len(rows) // 2)]
    return rows[0]


def kernel(Z, DP, H, factor, acts_hbm, grad_hbm, codes_hbm, scale_ref, col_ref, down_hbm, up_hbm,
           out_ref, gdown_ref, gup_ref,
           acts, grad, codes, weight, downf, upf, stage, mix, mix_t, low, terms,
           g1s, g1r, g2s, g2r, g3r, fin,
           load_sem, code_sem, down_sem, send_sem, w_sem, d_sem, u_sem, g1_sem, g2_sem, g3_sem, g4_sem):
    d, z = lax.axis_index("dp"), lax.axis_index("fsdp")
    p, core = lax.rem(d, GROUP), lax.rem(d, 2)
    xbit, ybit = lax.rem(d // 2, 2), lax.rem(d // 4, 2)
    dx, dy, ds_ = 2 - 4 * xbit, 4 - 8 * ybit, 1 - 2 * core
    rows, width = weight.shape[3], weight.shape[4]
    tile = H * rows
    per = GROUP // H
    shard = GROUP * tile
    R = mix.shape[1]
    RH = R // 2
    up_width = upf.shape[2]
    blocks = rows // 64
    near = jnp.minimum(z, Z - 1 - z)

    def source(k):
        paired = jnp.where(k % 2 == 0, z - (k // 2 + 1), z + (k // 2 + 1))
        rest = jnp.where(2 * z < Z - 1, z + (k - near + 1), z - (k - near + 1))
        return jnp.where(k < 2 * near, paired, rest)

    at_x, at_y, at_s, at_d = (d + dx, z), (d + dy, z), (d + ds_, z), (d + dx + dy, z)
    pairs = DP // 2
    others = [lax.rem(d + 2 * j, DP) for j in range(1, pairs)]

    code_loads = [
        pltpu.make_async_copy(codes_hbm.at[h * GROUP * blocks:(h + 1) * GROUP * blocks],
                              codes.at[h * GROUP * blocks:(h + 1) * GROUP * blocks], code_sem.at[h])
        for h in range(H)
    ]
    loads = [
        pltpu.make_async_copy(up_hbm, upf.at[z], load_sem.at[0]),
        pltpu.make_async_copy(grad_hbm, grad, load_sem.at[1]),
        pltpu.make_async_copy(acts_hbm, acts, load_sem.at[2]),
    ]
    down_loads = [
        pltpu.make_async_copy(down_hbm.at[:, q * tile:(q + 1) * tile], downf.at[z, q], down_sem.at[q])
        for q in range(GROUP)
    ]
    code_loads[0].start()
    loads[0].start()
    for c in down_loads:
        c.start()
    for c in code_loads[1:]:
        c.start()
    loads[1].start()
    loads[2].start()

    barrier = pltpu.get_barrier_semaphore()
    for k in range(Z - 1):
        pl.semaphore_signal(barrier, inc=1, device_id=(d, source(k)), device_id_type=MESH)
    for o in others:
        pl.semaphore_signal(barrier, inc=1, device_id=(o, z), device_id_type=MESH)
    pl.semaphore_signal(barrier, inc=1, device_id=at_s, device_id_type=MESH)

    sends, conditions = [], {}

    def send(src, dst, sem, to):
        c = pltpu.make_async_remote_copy(src_ref=src, dst_ref=dst, send_sem=send_sem.at[len(sends)],
                                         recv_sem=sem, device_id=to, device_id_type=MESH)
        c.start()
        sends.append(c)

    def send_if(on, src, dst, sem, to):
        c = pltpu.make_async_remote_copy(src_ref=src, dst_ref=dst, send_sem=send_sem.at[len(sends)],
                                         recv_sem=sem, device_id=to, device_id_type=MESH)
        pl.when(on)(c.start)
        sends.append(c)
        conditions[len(sends) - 1] = on

    def arrived(ref, sem):
        pltpu.make_async_remote_copy(src_ref=ref, dst_ref=ref, send_sem=send_sem.at[0], recv_sem=sem,
                                     device_id=at_s, device_id_type=MESH).wait_recv()

    def send_w(s, h, q, to):
        send(weight.at[s, h, q], weight.at[s, h, q], w_sem.at[s, h, q], to)

    def send_w_if(on, s, h, q, to):
        send_if(on, weight.at[s, h, q], weight.at[s, h, q], w_sem.at[s, h, q], to)

    def wait_w(s, h, q):
        arrived(weight.at[s, h, q], w_sem.at[s, h, q])

    def send_d(s, q, to):
        send(downf.at[s, q], downf.at[s, q], d_sem.at[s, q], to)

    def wait_d(s, q):
        arrived(downf.at[s, q], d_sem.at[s, q])

    def dequantize(h, q):
        for r in range(blocks):
            b = (h * GROUP + q) * blocks + r

            def columns(c, _, b=b, r=r):
                cols = pl.ds(pl.multiple_of(c * 256, 256), 256)
                words = codes[b, :, cols]
                absmax = (scale_ref[pl.ds(b, 1), cols].astype(jnp.float32) + 1.0) / 256.0 * col_ref[:, cols]
                for j in range(4):
                    stage[pl.ds(j, 16, stride=4), :] = levels_of(words, j)[:, :128] * absmax[:, :128]
                    stage[pl.ds(64 + j, 16, stride=4), :] = levels_of(words, j)[:, 128:] * absmax[:, 128:]
                weight[z, h, q, pl.ds(r * 64, 64), pl.ds(pl.multiple_of(c * 256, 128), 128)] = stage[0:64].astype(jnp.bfloat16)
                weight[z, h, q, pl.ds(r * 64, 64), pl.ds(pl.multiple_of(c * 256 + 128, 128), 128)] = stage[64:128].astype(jnp.bfloat16)
                return 0

            lax.fori_loop(0, width // 256, columns, 0)

    def tiles(s, h):
        def one(t, _):
            part = weight[s, h, pl.ds(H * t, H)].reshape(tile, width)
            tt = h * per + t
            acc = lax.dot_general(grad[...], part, NT, preferred_element_type=jnp.float32)
            acc += adapter_scale * jnp.dot(mix[...], downf[s, tt], preferred_element_type=jnp.float32)
            out_ref[:, pl.ds(pl.multiple_of((s * GROUP + tt) * tile, tile), tile)] = acc.astype(jnp.bfloat16)
            return 0

        lax.fori_loop(0, per, one, 0)

    px, py, ps = p + dx, p + dy, p + ds_
    pd = p + dx + dy
    same_core = (p, px, py, pd)
    events = H * (Z - 1)

    def event(i):
        pair, r = i // (2 * H), i % (2 * H)
        both = i // H < 2 * near
        k = jnp.where(both, 2 * pair + r % 2, i // H)
        h = jnp.where(both, r // 2, i % H)
        paired = jnp.where(k % 2 == 0, z - (k // 2 + 1), z + (k // 2 + 1))
        rest = jnp.where(2 * z < Z - 1, z + (k - near + 1), z - (k - near + 1))
        return jnp.where(both, paired, rest), h

    def passes_on(s):
        return ((s < z) & (z < Z - 1)) | ((s > z) & (z > 0))

    def at_end(s):
        return (s == 0) | (s == Z - 1)

    def onward(s, on):
        return d, jnp.where(on, z + jnp.where(s < z, 1, -1), source(0))

    def pass_on(i):
        s, h = event(i)
        on = passes_on(s)
        pl.when(on)(lambda: wait_w(s, h, p))
        send_w_if(on, s, h, p, onward(s, on))

    def first(i):
        s, h = event(i)
        pl.when(jnp.logical_not(passes_on(s)))(lambda: wait_w(s, h, p))
        send_w(s, h, p, at_x)
        send_w(s, h, p, at_y)
        send_w(s, h, p, at_s)

    def second(i):
        s, h = event(i)
        even = h % 2 == 0
        wait_w(s, h, px)
        wait_w(s, h, py)
        send_w_if(jnp.logical_not(at_end(s)), s, h, jnp.where(even, px, py), (d + jnp.where(even, dy, dx), z))
        send_w(s, h, px, at_s)
        send_w(s, h, py, at_s)

    def third(i):
        s, h = event(i)
        wait_w(s, h, pd)
        on = at_end(s) & passes_on(s)
        send_w_if(on, s, h, pd, onward(s, on))
        send_w(s, h, pd, at_s)

    def use(i):
        s, h = event(i)
        for q in same_core:
            wait_w(s, h, q + ds_)
        tiles(s, h)

    last = events - H
    second_at = {e: e + LAG1 for e in range(events)}
    third_at = {e: e + LAG1 if e >= last else min(e + LAG2, last + LAG1) for e in range(events)}

    def own(h):
        dequantize(h, px)
        send_w(z, h, px, at_s)
        dequantize(h, py)
        send_w(z, h, py, at_s)

    def own_use(h):
        for q in same_core:
            wait_w(z, h, q + ds_)
        tiles(z, h)

    code_loads[0].wait()
    dequantize(0, p)
    pl.semaphore_wait(barrier, (Z - 1) + (pairs - 1) + 1)
    loads[0].wait()
    for k in range(Z - 1):
        send(upf.at[z], upf.at[z], u_sem.at[z], (d, source(k)))
    for c in down_loads:
        c.wait()
    for k in range(Z - 1):
        send_d(z, p, (d, source(k)))
    for h in range(H):
        if h > 0:
            code_loads[h].wait()
            dequantize(h, p)
        send_w_if(z < Z - 1, z, h, p, (d, jnp.where(z < Z - 1, z + 1, z - 1)))
        send_w_if(z > 0, z, h, p, (d, jnp.where(z > 0, z - 1, z + 1)))
        send_w(z, h, p, at_s)

    def own_far(h):
        dequantize(h, pd)
        send_w_if(at_end(z), z, h, pd, (d, jnp.where(z == 0, z + 1, z - 1)))
        send_w(z, h, pd, at_s)

    def mixed():
        loads[1].wait()
        for k in range(Z - 1):
            arrived(upf.at[source(k)], u_sem.at[source(k)])
        total = jnp.zeros(mix.shape, jnp.float32)
        for s in range(Z):
            total += lax.dot_general(grad[:, s * up_width:(s + 1) * up_width], upf[s], NT,
                                     preferred_element_type=jnp.float32)
        mix[...] = total.astype(jnp.bfloat16)
        mix_t[...] = total.astype(jnp.bfloat16).astype(jnp.float32).T.astype(jnp.bfloat16)

    def down_first():
        for k in range(Z - 1):
            s = source(k)
            wait_d(s, p)
            for to in (at_x, at_y, at_d, at_s):
                send_d(s, p, to)

    def down_second():
        for k in range(Z - 1):
            s = source(k)
            for q in (px, py, pd):
                wait_d(s, q)
                send_d(s, q, at_s)

    def down_third():
        for k in range(Z - 1):
            for q in same_core:
                wait_d(source(k), q + ds_)

    def products(k):
        s = z if k < 0 else source(k)
        if k < 0:
            loads[2].wait()

        def one(q, total):
            t = s * GROUP + q
            a = acts[:, pl.ds(pl.multiple_of(t * tile, tile), tile)]
            terms[s, :, pl.ds(pl.multiple_of(q * tile, tile), tile)] = jnp.dot(
                mix_t[...], a, preferred_element_type=jnp.float32)
            return total + lax.dot_general(a, downf[s, q], NT, preferred_element_type=jnp.float32)

        begin = jnp.zeros(mix.shape, jnp.float32) if k < 0 else low[...]
        low[...] = lax.fori_loop(0, GROUP, one, begin)

    def gradient_terms():
        low_t = low[...].astype(jnp.bfloat16).astype(jnp.float32).T.astype(jnp.bfloat16)
        for s in range(Z):
            terms[s, :, shard:shard + up_width] = jnp.dot(
                low_t, grad[:, s * up_width:(s + 1) * up_width], preferred_element_type=jnp.float32)
        theirs = pl.multiple_of((1 - core) * RH, RH)
        for s in range(Z):
            g1s[s] = terms[s, pl.ds(theirs, RH), :].astype(jnp.bfloat16)
        send(g1s, g1r, g1_sem.at[0], at_s)

    def reduce_core():
        arrived(g1r, g1_sem.at[0])
        mine = pl.multiple_of(core * RH, RH)
        for s in range(Z):
            total = terms[s, pl.ds(mine, RH), :] + g1r[s].astype(jnp.float32)
            terms[s, pl.ds(mine, RH), :] = total
            g2s[s] = total.astype(jnp.bfloat16)
        for k in range(Z - 1):
            s = source(k)
            send(g2s.at[s], g2r.at[z], g2_sem.at[z], (d, s))

    def reduce_fsdp():
        mine = pl.multiple_of(core * RH, RH)
        total = terms[z, pl.ds(mine, RH), :]
        for k in range(Z - 1):
            s = source(k)
            arrived(g2r.at[s], g2_sem.at[s])
            total += g2r[s].astype(jnp.float32)
        slot = d // 2
        g3r[slot] = total.astype(jnp.bfloat16)
        for o in others:
            send(g3r.at[slot], g3r.at[slot], g3_sem.at[slot], (o, z))

    def reduce_dp():
        for o in others:
            arrived(g3r.at[o // 2], g3_sem.at[o // 2])
        total = g3r[0].astype(jnp.float32)
        for j in range(1, pairs):
            total += g3r[j].astype(jnp.float32)
        fin[core] = factor * total
        send(fin.at[core], fin.at[core], g4_sem.at[0], at_s)

    def finish():
        arrived(fin.at[1 - core], g4_sem.at[0])
        for c in range(2):
            gdown_ref[c * RH:(c + 1) * RH, :] = fin[c, :, :shard]
            gup_ref[c * RH:(c + 1) * RH, :] = fin[c, :, shard:shard + up_width]

    for h in range(H):
        own_far(h)
    mixed()
    down_first()
    products(-1)
    work = [
        [down_second, lambda: own(0)],
        [down_third] + [lambda h=h: own(h) for h in range(1, H)],
    ]
    work += [[lambda k=k: products(k)] for k in range(Z - 1)]
    work[-1].append(gradient_terms)
    work += [[lambda: own_use(0)]]
    work += [[reduce_core, lambda: own_use(1)]]
    work += [[lambda h=h: own_use(h)] for h in range(2, H)]
    work += [[reduce_fsdp], [], [reduce_dp], [], [finish]]

    for i in range(max(events + LAG1 + 1, len(work))):
        if i == 0:
            pass_on(0)
        if i < events:
            first(i)
        for j in range(1, AHEAD + 1) if i == 0 else [i + AHEAD]:
            if j < events:
                pass_on(j)
        for e in range(events):
            if second_at[e] == i:
                second(e)
        for e in range(events):
            if third_at[e] == i:
                third(e)
        for e in range(events):
            if third_at[e] == i - 1:
                use(e)
        if i < len(work):
            for step in work[i]:
                step()

    for j, c in enumerate(sends):
        if j in conditions:
            pl.when(conditions[j])(c.wait_send)
        else:
            c.wait_send()


def solution(mesh):
    Z, DP = mesh.shape["fsdp"], mesh.shape["dp"]
    bf16, f32 = jnp.bfloat16, jnp.float32

    def local(acts, grad_out, codes, scale_codes, col_scale, down_adapter, up_adapter):
        tokens, D = acts.shape
        O = grad_out.shape[1]
        R, shard = down_adapter.shape
        up_width = up_adapter.shape[1]
        tile = shard // GROUP
        wide = shard + up_width
        RH = R // 2
        factor = adapter_scale * float(tokens * Z * DP) ** (-0.5)
        blocks = codes.shape[0]
        H = max(1, blocks // GROUP)
        n_sends = 7 * H + (Z - 1) * (2 + 7 + 9 * H + 1) + 1 + (DP // 2 - 1) + 1
        DMA = pltpu.SemaphoreType.DMA
        anywhere, vmem = pl.BlockSpec(memory_space=pl.ANY), pl.BlockSpec(memory_space=pltpu.VMEM)
        return pl.pallas_call(
            functools.partial(kernel, Z, DP, H, factor),
            out_shape=(
                pltpu.VMEM((tokens, D), bf16),
                pltpu.VMEM((R, shard), f32),
                pltpu.VMEM((R, up_width), f32),
            ),
            in_specs=[anywhere, anywhere, anywhere, vmem, vmem, anywhere, anywhere],
            out_specs=(vmem, vmem, vmem),
            scratch_shapes=[
                pltpu.VMEM((tokens, D), bf16),
                pltpu.VMEM((tokens, O), bf16),
                pltpu.VMEM(codes.shape, jnp.int32),
                pltpu.VMEM((Z, H, GROUP, tile // H, O), bf16),
                pltpu.VMEM((Z, GROUP, R, tile), bf16),
                pltpu.VMEM((Z, R, up_width), bf16),
                pltpu.VMEM((128, 128), f32),
                pltpu.VMEM((tokens, R), bf16),
                pltpu.VMEM((R, tokens), bf16),
                pltpu.VMEM((tokens, R), f32),
                pltpu.VMEM((Z, R, wide), f32),
                pltpu.VMEM((Z, RH, wide), bf16),
                pltpu.VMEM((Z, RH, wide), bf16),
                pltpu.VMEM((Z, RH, wide), bf16),
                pltpu.VMEM((Z, RH, wide), bf16),
                pltpu.VMEM((DP // 2, RH, wide), bf16),
                pltpu.VMEM((2, RH, wide), f32),
                DMA((3,)), DMA((H,)), DMA((GROUP,)), DMA((n_sends,)),
                DMA((Z, H, GROUP)), DMA((Z, GROUP)), DMA((Z,)),
                DMA((1,)), DMA((Z,)), DMA((DP // 2,)), DMA((1,)),
            ],
            compiler_params=pltpu.CompilerParams(
                collective_id=0, has_side_effects=True, vmem_limit_bytes=52 * 1024 * 1024
            ),
        )(acts, grad_out, codes, scale_codes, col_scale.reshape(1, -1), down_adapter, up_adapter)

    placed = (
        P(("dp", "fsdp"), None),
        P(("dp", "fsdp"), None),
        P("fsdp", None, None),
        P("fsdp", None),
        P(),
        P(None, "fsdp"),
        P(None, "fsdp"),
    )
    return jax.shard_map(
        local,
        mesh=mesh,
        in_specs=placed,
        out_specs=(P(("dp", "fsdp"), None), P(None, "fsdp"), P(None, "fsdp")),
        check_vma=False,
    )
```

```python
import functools

import jax
import jax.numpy as jnp
from jax import lax
from jax.experimental import pallas as pl
from jax.experimental.pallas import tpu as pltpu
from jax.sharding import PartitionSpec as P

MESH = pl.DeviceIdType.MESH
NT = (((1,), (1,)), ((), ()))
adapter_scale = 0.5
nf4_table = [
    -1.0,
    -0.6961928009986877,
    -0.5250730514526367,
    -0.39491748809814453,
    -0.28444138169288635,
    -0.18477343022823334,
    -0.09105003625154495,
    0.0,
    0.07958029955625534,
    0.16093020141124725,
    0.24611230194568634,
    0.33791524171829224,
    0.44070982933044434,
    0.5626170039176941,
    0.7229568362236023,
    1.0,
]
GROUP = 8
STRIPES = 8
LATE = 5
SECOND = (2, 2, 3, 3, 2, 3, 2, 3, 3, 6, 7, 7)
THIRD = (5, 4, 7, 6, 9, 8, 8, 9, 8, 8, 8, 7)
FAR = (3, 3, 4, 3, 4, 4, 4, 3, 2, 2, 1, 6)
AHEAD = (0, 1, 1, 1, 2, 2, 3, 3, 4, 4, 3, 2)
PRODUCTS = (1, 2, 3, 4)
DEQUANT = (3, 4, 5, 7)
OWN = (6, 6, 9, 13)
CHAIN = (6, 9, 9)
MIX, DOWN, CORE, HOME, SPREAD, GATHER = (0, 0, 5, 10, 16, 18)


def spread(table, n):
    return [table[i * len(table) // n] for i in range(n)]


def levels_of(words, nibble):
    rows = [jnp.float32(v) for v in nf4_table]
    for bit in range(4):
        on = (words & (1 << (4 * nibble + bit))) != 0
        rows = [jnp.where(on, rows[2 * i + 1], rows[2 * i]) for i in range(len(rows) // 2)]
    return rows[0]


def kernel(Z, DP, H, factor, acts_hbm, grad_hbm, codes_hbm, scale_ref, col_ref, down_hbm, up_hbm,
           out_ref, gdown_ref, gup_ref,
           acts, grad, codes, weight, downf, upf, stage, mix, mix_t, low, terms,
           g1s, g1r, g2s, g2r, g3s, g3r, g4, fin,
           load_sem, code_sem, down_sem, send_sem, w_sem, d_sem, u_sem, g1_sem, g2_sem, g3_sem, g4_sem, fin_sem):
    d, z = lax.axis_index("dp"), lax.axis_index("fsdp")
    core = lax.rem(d, 2)
    side = GROUP // 2
    p = side * core + lax.rem(d // 2, side)
    xbit, ybit = lax.rem(d // 2, 2), lax.rem(d // 4, 2)
    dx, dy, ds_ = 2 - 4 * xbit, 4 - 8 * ybit, 1 - 2 * core
    rows, width = weight.shape[3], weight.shape[4]
    tile = H * rows
    per = GROUP // H
    shard = GROUP * tile
    R = mix.shape[1]
    RH = R // 2
    up_width = upf.shape[2]
    blocks = rows // 64
    near = jnp.minimum(z, Z - 1 - z)

    def source(k):
        paired = jnp.where(k % 2 == 0, z - (k // 2 + 1), z + (k // 2 + 1))
        rest = jnp.where(2 * z < Z - 1, z + (k - near + 1), z - (k - near + 1))
        return jnp.where(k < 2 * near, paired, rest)

    mine = pl.ds(pl.multiple_of(core * RH, RH), RH)
    part, columns = g4.shape[1], g4.shape[2]
    at_x, at_y, at_s, at_d = (d + dx, z), (d + dy, z), (d + ds_, z), (d + dx + dy, z)
    pairs = DP // 2
    others = [lax.rem(d + 2 * j, DP) for j in range(1, pairs)]

    code_loads = [
        pltpu.make_async_copy(codes_hbm.at[h * GROUP * blocks:(h + 1) * GROUP * blocks],
                              codes.at[h * GROUP * blocks:(h + 1) * GROUP * blocks], code_sem.at[h])
        for h in range(H)
    ]
    loads = [
        pltpu.make_async_copy(up_hbm, upf.at[z], load_sem.at[0]),
        pltpu.make_async_copy(grad_hbm, grad, load_sem.at[1]),
        pltpu.make_async_copy(acts_hbm, acts, load_sem.at[2]),
    ]
    down_loads = [
        pltpu.make_async_copy(down_hbm.at[:, q * tile:(q + 1) * tile], downf.at[z, q], down_sem.at[q])
        for q in range(GROUP)
    ]
    code_loads[0].start()
    loads[0].start()
    for c in down_loads:
        c.start()
    for c in code_loads[1:]:
        c.start()
    loads[1].start()
    loads[2].start()

    barrier = pltpu.get_barrier_semaphore()
    for k in range(Z - 1):
        pl.semaphore_signal(barrier, inc=1, device_id=(d, source(k)), device_id_type=MESH)
    for o in others:
        pl.semaphore_signal(barrier, inc=1, device_id=(o, z), device_id_type=MESH)
    pl.semaphore_signal(barrier, inc=1, device_id=at_s, device_id_type=MESH)

    sends, conditions = [], {}

    def send(src, dst, sem, to):
        c = pltpu.make_async_remote_copy(src_ref=src, dst_ref=dst, send_sem=send_sem.at[len(sends)],
                                         recv_sem=sem, device_id=to, device_id_type=MESH)
        c.start()
        sends.append(c)

    def send_if(on, src, dst, sem, to):
        c = pltpu.make_async_remote_copy(src_ref=src, dst_ref=dst, send_sem=send_sem.at[len(sends)],
                                         recv_sem=sem, device_id=to, device_id_type=MESH)
        pl.when(on)(c.start)
        sends.append(c)
        conditions[len(sends) - 1] = on

    def arrived(ref, sem):
        pltpu.make_async_remote_copy(src_ref=ref, dst_ref=ref, send_sem=send_sem.at[0], recv_sem=sem,
                                     device_id=at_s, device_id_type=MESH).wait_recv()

    def send_w(s, h, q, to):
        send(weight.at[s, h, q], weight.at[s, h, q], w_sem.at[s, h, q], to)

    def send_w_if(on, s, h, q, to):
        send_if(on, weight.at[s, h, q], weight.at[s, h, q], w_sem.at[s, h, q], to)

    def wait_w(s, h, q):
        arrived(weight.at[s, h, q], w_sem.at[s, h, q])

    def share_w(s, h):
        piece = weight.at[s, h, pl.ds(here, side)]
        send(piece, piece, w_sem.at[s, h, here], at_s)

    def await_w(s, h):
        arrived(weight.at[s, h, pl.ds(there, side)], w_sem.at[s, h, there])

    def send_d(s, q, to):
        send(downf.at[s, q], downf.at[s, q], d_sem.at[s, q], to)

    def wait_d(s, q):
        arrived(downf.at[s, q], d_sem.at[s, q])

    def dequantize(h, q):
        for r in range(blocks):
            b = (h * GROUP + q) * blocks + r

            def columns(c, _, b=b, r=r):
                cols = pl.ds(pl.multiple_of(c * 256, 256), 256)
                words = codes[b, :, cols]
                absmax = (scale_ref[pl.ds(b, 1), cols].astype(jnp.float32) + 1.0) / 256.0 * col_ref[:, cols]
                for j in range(4):
                    stage[pl.ds(j, 16, stride=4), :] = levels_of(words, j)[:, :128] * absmax[:, :128]
                    stage[pl.ds(64 + j, 16, stride=4), :] = levels_of(words, j)[:, 128:] * absmax[:, 128:]
                weight[z, h, q, pl.ds(r * 64, 64), pl.ds(pl.multiple_of(c * 256, 128), 128)] = stage[0:64].astype(jnp.bfloat16)
                weight[z, h, q, pl.ds(r * 64, 64), pl.ds(pl.multiple_of(c * 256 + 128, 128), 128)] = stage[64:128].astype(jnp.bfloat16)
                return 0

            lax.fori_loop(0, width // 256, columns, 0)

    def tiles(s, h):
        def one(t, _):
            part = weight[s, h, pl.ds(H * t, H)].reshape(tile, width)
            tt = h * per + t
            acc = lax.dot_general(grad[...], part, NT, preferred_element_type=jnp.float32)
            acc += adapter_scale * jnp.dot(mix[...], downf[s, tt], preferred_element_type=jnp.float32)
            out_ref[:, pl.ds(pl.multiple_of((s * GROUP + tt) * tile, tile), tile)] = acc.astype(jnp.bfloat16)
            return 0

        lax.fori_loop(0, per, one, 0, unroll=2)

    px, py = p + 1 - 2 * xbit, p + 2 - 4 * ybit
    pd = px + py - p
    here, there = pl.multiple_of(side * core, side), pl.multiple_of(side * (1 - core), side)
    events = H * (Z - 1)

    def event(i):
        pair, r = i // (2 * H), i % (2 * H)
        both = i // H < 2 * near
        k = jnp.where(both, 2 * pair + r % 2, i // H)
        h = jnp.where(both, r // 2, i % H)
        paired = jnp.where(k % 2 == 0, z - (k // 2 + 1), z + (k // 2 + 1))
        rest = jnp.where(2 * z < Z - 1, z + (k - near + 1), z - (k - near + 1))
        return jnp.where(both, paired, rest), h

    def passes_on(s):
        return ((s < z) & (z < Z - 1)) | ((s > z) & (z > 0))

    def at_end(s):
        return (s == 0) | (s == Z - 1)

    def onward(s, on):
        return d, jnp.where(on, z + jnp.where(s < z, 1, -1), source(0))

    def pass_on(i):
        s, h = event(i)
        on = passes_on(s)
        pl.when(on)(lambda: wait_w(s, h, p))
        send_w_if(on, s, h, p, onward(s, on))

    def first(i):
        s, h = event(i)
        pl.when(jnp.logical_not(passes_on(s)))(lambda: wait_w(s, h, p))
        send_w(s, h, p, at_x)
        send_w(s, h, p, at_y)

    def second(i):
        s, h = event(i)
        even = h % 2 == 0
        wait_w(s, h, px)
        wait_w(s, h, py)
        send_w_if(jnp.logical_not(at_end(s)), s, h, jnp.where(even, px, py), (d + jnp.where(even, dy, dx), z))

    def third(i):
        s, h = event(i)
        pl.when(jnp.logical_not(at_end(s) & passes_on(s)))(lambda: wait_w(s, h, pd))
        share_w(s, h)

    def pass_far(i):
        s, h = event(i)
        on = at_end(s) & passes_on(s)
        pl.when(on)(lambda: wait_w(s, h, pd))
        send_w_if(on, s, h, pd, onward(s, on))

    def use(i):
        s, h = event(i)
        await_w(s, h)
        tiles(s, h)

    second_at, third_at, ahead_at, far_at = [], [], [], []
    tables = zip(*(spread(table, events) for table in (SECOND, THIRD, AHEAD, FAR)))
    for e, (lag2, lag3, lead, far) in enumerate(tables):
        second_at.append(max([e + lag2] + second_at[-1:]))
        third_at.append(max([e + lag3, second_at[e]] + third_at[-1:]))
        far_at.append(max([e + far] + far_at[-1:]))
        ahead_at.append(max([0, e - lead] + ahead_at[-1:]))

    def own(h):
        dequantize(h, px)
        dequantize(h, py)
        share_w(z, h)

    def own_use(h):
        await_w(z, h)
        tiles(z, h)

    def own_near(h):
        send_w_if(z < Z - 1, z, h, p, (d, jnp.where(z < Z - 1, z + 1, z - 1)))
        send_w_if(z > 0, z, h, p, (d, jnp.where(z > 0, z - 1, z + 1)))

    code_loads[0].wait()
    dequantize(0, p)
    pl.semaphore_wait(barrier, (Z - 1) + (pairs - 1) + 1)
    for c in down_loads:
        c.wait()
    for k in range(Z - 1):
        send_d(z, p, (d, source(k)))
    own_near(0)
    loads[0].wait()
    half = pl.ds(pl.multiple_of(core * RH, RH), RH)
    for k in range(Z - 1):
        send(upf.at[z, half], upf.at[z, half], u_sem.at[z, core], (d, source(k)))
    for h in range(1, H):
        code_loads[h].wait()
        dequantize(h, p)
        own_near(h)

    def own_far(h):
        dequantize(h, pd)
        send_w_if(at_end(z), z, h, pd, (d, jnp.where(z == 0, z + 1, z - 1)))

    def mixed():
        loads[1].wait()
        for k in range(Z - 1):
            piece = upf.at[source(k), half]
            arrived(piece, u_sem.at[source(k), core])
            send(piece, piece, u_sem.at[source(k), core], at_s)
        for k in range(Z - 1):
            arrived(upf.at[source(k), half], u_sem.at[source(k), 1 - core])
        total = jnp.zeros(mix.shape, jnp.float32)
        for s in range(Z):
            total += lax.dot_general(grad[:, s * up_width:(s + 1) * up_width], upf[s], NT,
                                     preferred_element_type=jnp.float32)
        mix[...] = total.astype(jnp.bfloat16)
        mix_t[...] = total.astype(jnp.bfloat16).astype(jnp.float32).T.astype(jnp.bfloat16)

    def down_first():
        for k in range(Z - 1):
            s = source(k)
            wait_d(s, p)
            for to in (at_x, at_y):
                send_d(s, p, to)

    def down_second():
        for k in range(Z - 1):
            s = source(k)
            for q in (px, py):
                wait_d(s, q)
            send_d(s, *((px, at_y) if k % 2 == 0 else (py, at_x)))

    def down_share():
        for k in range(Z - 1):
            s = source(k)
            wait_d(s, pd)
            piece = downf.at[s, pl.ds(here, side)]
            send(piece, piece, d_sem.at[s, here], at_s)

    def down_third():
        for k in range(Z - 1):
            arrived(downf.at[source(k), pl.ds(there, side)], d_sem.at[source(k), there])

    def products(k):
        s = z if k < 0 else source(k)
        if k < 0:
            loads[2].wait()

        def one(q, total):
            t = s * GROUP + q
            a = acts[:, pl.ds(pl.multiple_of(t * tile, tile), tile)]
            terms[s, :, pl.ds(pl.multiple_of(q * tile, tile), tile)] = jnp.dot(
                mix_t[...], a, preferred_element_type=jnp.float32)
            return total + lax.dot_general(a, downf[s, q], NT, preferred_element_type=jnp.float32)

        begin = jnp.zeros(mix.shape, jnp.float32) if k < 0 else low[...]
        low[...] = lax.fori_loop(0, GROUP, one, begin)

    def gradient_terms():
        low_t = low[...].astype(jnp.bfloat16).astype(jnp.float32).T.astype(jnp.bfloat16)
        for s in range(Z):
            terms[s, :, shard:shard + up_width] = jnp.dot(
                low_t, grad[:, s * up_width:(s + 1) * up_width], preferred_element_type=jnp.float32)
        if terms.shape[2] > shard + up_width:
            terms[:, :, shard + up_width:] = jnp.zeros((Z, R, terms.shape[2] - shard - up_width), jnp.float32)
        theirs = pl.multiple_of((1 - core) * RH, RH)
        for s in range(Z):
            g1s[s] = terms[s, pl.ds(theirs, RH), :].astype(jnp.bfloat16)
        send(g1s, g1r, g1_sem.at[0], at_s)

    def reduce_core():
        arrived(g1r, g1_sem.at[0])
        for s in range(Z):
            terms[s, mine, :] += g1r[s].astype(jnp.float32)

    edge = (z == 0) | (z == Z - 1)

    def chain(k, on):
        s = source(Z - 2 - k)
        down = s < z
        way = jnp.where(down, 0, 1)

        def add():
            terms[s, mine, :] += g2r[way, s].astype(jnp.float32)

        def pack():
            g2s[s] = terms[s, mine, :].astype(jnp.bfloat16)

        if on is not edge:
            pl.when(on)(lambda: arrived(g2r.at[way, s], g2_sem.at[way, s]))
            pl.when(on)(add)
        pl.when(on)(pack)
        send_if(on, g2s.at[s], g2r.at[way, s], g2_sem.at[way, s], (d, z + jnp.where(down, -1, 1)))

    def chain_ends():
        for k in range(Z - 1):
            chain(k, edge)

    slot = d // 2

    def home():
        for way, on in ((0, z < Z - 1), (1, z > 0)):
            def add(way=way):
                arrived(g2r.at[way, z], g2_sem.at[way, z])
                terms[z, mine, :] += g2r[way, z].astype(jnp.float32)

            pl.when(on)(add)
        total = terms[z, mine, :].astype(jnp.bfloat16)
        for j in range(pairs):
            g3s[j] = total[j % 2 * part:(j % 2 + 1) * part, j // 2 * columns:(j // 2 + 1) * columns]
        for o in others:
            send(g3s.at[o // 2], g3r.at[slot], g3_sem.at[slot], (o, z))

    def reduce_dp():
        total = g3s[slot].astype(jnp.float32)
        for o in others:
            arrived(g3r.at[o // 2], g3_sem.at[o // 2])
            total += g3r[o // 2].astype(jnp.float32)
        g4[slot] = total.astype(jnp.bfloat16)
        for o in others:
            send(g4.at[slot], g4.at[slot], g4_sem.at[slot], (o, z))

    def gather_dp():
        for o in others:
            arrived(g4.at[o // 2], g4_sem.at[o // 2])
        for j in range(pairs):
            fin[core, j % 2 * part:(j % 2 + 1) * part, j // 2 * columns:(j // 2 + 1) * columns] = factor * g4[j].astype(jnp.float32)
        send(fin.at[core], fin.at[core], fin_sem.at[0], at_s)

    def finish():
        arrived(fin.at[1 - core], fin_sem.at[0])
        for c in range(2):
            gdown_ref[c * RH:(c + 1) * RH, :] = fin[c, :, :shard]
            gup_ref[c * RH:(c + 1) * RH, :] = fin[c, :, shard:shard + up_width]

    for h in range(max(1, H - 2)):
        own_far(h)
    down_first()
    for h in range(max(1, H - 2), H):
        own_far(h)

    work = [[] for _ in range(GATHER + events)]
    work[DOWN].append(down_second)
    work[MIX].append(mixed)
    for k, i in enumerate(spread(PRODUCTS, Z)):
        if k == 1:
            work[i].extend([down_share, down_third])
        work[i].append(lambda k=k: products(k - 1))
    work[PRODUCTS[-1]].append(gradient_terms)
    for h, i in enumerate(spread(DEQUANT, H)):
        work[i].append(lambda h=h: own(h))
    for h, i in enumerate(spread(OWN, H)):
        work[i].append(lambda h=h: own_use(h))
    work[CORE].append(reduce_core)
    work[CORE].append(chain_ends)
    for k, i in enumerate(spread(CHAIN, Z - 1)):
        work[i].append(lambda k=k: chain(k, jnp.logical_not(edge)))
    work[HOME].append(home)
    work[SPREAD].append(reduce_dp)
    work[GATHER].append(gather_dp)
    work[GATHER + 1].append(finish)

    issued, drained = [], [0]

    def drain(upto):
        for j in range(drained[0], upto):
            if j in conditions:
                pl.when(conditions[j])(sends[j].wait_send)
            else:
                sends[j].wait_send()
        drained[0] = upto

    for i in range(len(work)):
        if i == 0:
            pass_on(0)
        if i < events:
            first(i)
        for e in range(1, events):
            if ahead_at[e] == i:
                pass_on(e)
        for e in range(events):
            if second_at[e] == i:
                second(e)
        for e in range(events):
            if far_at[e] == i:
                pass_far(e)
        for e in range(events):
            if third_at[e] == i:
                third(e)
        for e in range(events):
            if third_at[e] == i - 1:
                use(e)
        for step in work[i]:
            step()
        issued.append(len(sends))
        if i >= LATE:
            drain(issued[i - LATE])

    drain(len(sends))


def write_out(held, gdown_held, gup_held, out_hbm, gdown_hbm, gup_hbm, sem):
    rows = held.shape[0] // STRIPES
    copies = [
        pltpu.make_async_copy(held.at[i * rows:(i + 1) * rows], out_hbm.at[i * rows:(i + 1) * rows], sem.at[i])
        for i in range(STRIPES)
    ]
    copies += [
        pltpu.make_async_copy(gdown_held, gdown_hbm, sem.at[STRIPES]),
        pltpu.make_async_copy(gup_held, gup_hbm, sem.at[STRIPES + 1]),
    ]
    for c in copies:
        c.start()
    for c in copies:
        c.wait()


def solution(mesh):
    Z, DP = mesh.shape["fsdp"], mesh.shape["dp"]
    bf16, f32 = jnp.bfloat16, jnp.float32

    def local(acts, grad_out, codes, scale_codes, col_scale, down_adapter, up_adapter):
        tokens, D = acts.shape
        O = grad_out.shape[1]
        R, shard = down_adapter.shape
        up_width = up_adapter.shape[1]
        tile = shard // GROUP
        wide = shard + up_width
        RH = R // 2
        factor = adapter_scale * float(tokens * Z * DP) ** (-0.5)
        blocks = codes.shape[0]
        H = max(1, blocks // GROUP)
        pairs = DP // 2
        part = RH // 2
        columns = -(-wide // (pairs // 2 * 128)) * 128
        wide = columns * (pairs // 2)
        n_sends = 4 * H + (Z - 1) * (3 + 4 + 6 * H + 2) + 1 + 2 * (pairs - 1) + 1
        DMA = pltpu.SemaphoreType.DMA
        anywhere, vmem = pl.BlockSpec(memory_space=pl.ANY), pl.BlockSpec(memory_space=pltpu.VMEM)
        held = pl.pallas_call(
            functools.partial(kernel, Z, DP, H, factor),
            out_shape=(
                pltpu.VMEM((tokens, D), bf16),
                pltpu.VMEM((R, shard), f32),
                pltpu.VMEM((R, up_width), f32),
            ),
            in_specs=[anywhere, anywhere, anywhere, vmem, vmem, anywhere, anywhere],
            out_specs=(vmem, vmem, vmem),
            scratch_shapes=[
                pltpu.VMEM((tokens, D), bf16),
                pltpu.VMEM((tokens, O), bf16),
                pltpu.VMEM(codes.shape, jnp.int32),
                pltpu.VMEM((Z, H, GROUP, tile // H, O), bf16),
                pltpu.VMEM((Z, GROUP, R, tile), bf16),
                pltpu.VMEM((Z, R, up_width), bf16),
                pltpu.VMEM((128, 128), f32),
                pltpu.VMEM((tokens, R), bf16),
                pltpu.VMEM((R, tokens), bf16),
                pltpu.VMEM((tokens, R), f32),
                pltpu.VMEM((Z, R, wide), f32),
                pltpu.VMEM((Z, RH, wide), bf16),
                pltpu.VMEM((Z, RH, wide), bf16),
                pltpu.VMEM((Z, RH, wide), bf16),
                pltpu.VMEM((2, Z, RH, wide), bf16),
                pltpu.VMEM((pairs, part, columns), bf16),
                pltpu.VMEM((pairs, part, columns), bf16),
                pltpu.VMEM((pairs, part, columns), bf16),
                pltpu.VMEM((2, RH, wide), f32),
                DMA((3,)), DMA((H,)), DMA((GROUP,)), DMA((n_sends,)),
                DMA((Z, H, GROUP)), DMA((Z, GROUP)), DMA((Z, 2)),
                DMA((1,)), DMA((2, Z)), DMA((pairs,)), DMA((pairs,)), DMA((1,)),
            ],
            compiler_params=pltpu.CompilerParams(
                collective_id=0, has_side_effects=True, vmem_limit_bytes=52 * 1024 * 1024
            ),
        )(acts, grad_out, codes, scale_codes, col_scale.reshape(1, -1), down_adapter, up_adapter)
        return pl.pallas_call(
            write_out,
            out_shape=(
                jax.ShapeDtypeStruct((tokens, D), bf16),
                jax.ShapeDtypeStruct((R, shard), f32),
                jax.ShapeDtypeStruct((R, up_width), f32),
            ),
            in_specs=[vmem] * 3,
            out_specs=(anywhere,) * 3,
            scratch_shapes=[DMA((STRIPES + 2,))],
            compiler_params=pltpu.CompilerParams(vmem_limit_bytes=1024 * 1024),
        )(*[pltpu.with_memory_space_constraint(x, pltpu.VMEM) for x in held])

    placed = (
        P(("dp", "fsdp"), None),
        P(("dp", "fsdp"), None),
        P("fsdp", None, None),
        P("fsdp", None),
        P(),
        P(None, "fsdp"),
        P(None, "fsdp"),
    )
    return jax.shard_map(
        local,
        mesh=mesh,
        in_specs=placed,
        out_specs=(P(("dp", "fsdp"), None), P(None, "fsdp"), P(None, "fsdp")),
        check_vma=False,
    )
```

```python
import functools

import jax
import jax.numpy as jnp
from jax import lax
from jax.experimental import pallas as pl
from jax.experimental.pallas import tpu as pltpu
from jax.sharding import PartitionSpec as P

MESH = pl.DeviceIdType.MESH
NT = (((1,), (1,)), ((), ()))
adapter_scale = 0.5
nf4_table = [
    -1.0,
    -0.6961928009986877,
    -0.5250730514526367,
    -0.39491748809814453,
    -0.28444138169288635,
    -0.18477343022823334,
    -0.09105003625154495,
    0.0,
    0.07958029955625534,
    0.16093020141124725,
    0.24611230194568634,
    0.33791524171829224,
    0.44070982933044434,
    0.5626170039176941,
    0.7229568362236023,
    1.0,
]
GROUP = 8
STRIPES = 8
LATE = 8
SECOND = (2, 2, 3, 3, 2, 3, 2, 3, 3, 6, 7, 7)
THIRD = (5, 4, 7, 6, 9, 8, 8, 9, 8, 8, 8, 7)
FAR = (3, 3, 4, 3, 4, 4, 4, 3, 2, 2, 1, 6)
AHEAD = (0, 1, 1, 1, 2, 2, 3, 3, 4, 4, 3, 2)
PRODUCTS = (1, 2, 3, 4)
DEQUANT = (3, 4, 5, 7)
OWN = (6, 6, 9, 13)
CHAIN = (6, 9, 9)
MIX, DOWN, CORE, HOME, SPREAD, GATHER = (0, 0, 5, 10, 16, 18)


def spread(table, n):
    return [table[i * len(table) // n] for i in range(n)]


def levels_of(words, nibble):
    rows = [jnp.float32(v) for v in nf4_table]
    for bit in range(4):
        on = (words & (1 << (4 * nibble + bit))) != 0
        rows = [jnp.where(on, rows[2 * i + 1], rows[2 * i]) for i in range(len(rows) // 2)]
    return rows[0]


def kernel(Z, DP, H, factor, acts_hbm, grad_hbm, codes_hbm, scale_hbm, col_hbm, down_hbm, up_hbm,
           out_ref, gdown_ref, gup_ref,
           acts, grad, codes, scale_ref, col_ref, weight, downf, upf, stage, mix, mix_t, low, terms,
           g1s, g1r, g2s, g2r, g3s, g3r, g4, fin,
           load_sem, code_sem, down_sem, send_sem, w_sem, d_sem, u_sem, g1_sem, g2_sem, g3_sem, g4_sem, fin_sem):
    d, z = lax.axis_index("dp"), lax.axis_index("fsdp")
    core = lax.rem(d, 2)
    side = GROUP // 2
    p = side * core + lax.rem(d // 2, side)
    xbit, ybit = lax.rem(d // 2, 2), lax.rem(d // 4, 2)
    dx, dy, ds_ = 2 - 4 * xbit, 4 - 8 * ybit, 1 - 2 * core
    rows, width = weight.shape[3], weight.shape[4]
    tile = H * rows
    per = GROUP // H
    shard = GROUP * tile
    R = mix.shape[1]
    RH = R // 2
    up_width = upf.shape[2]
    blocks = rows // 64
    near = jnp.minimum(z, Z - 1 - z)

    def source(k):
        paired = jnp.where(k % 2 == 0, z - (k // 2 + 1), z + (k // 2 + 1))
        rest = jnp.where(2 * z < Z - 1, z + (k - near + 1), z - (k - near + 1))
        return jnp.where(k < 2 * near, paired, rest)

    mine = pl.ds(pl.multiple_of(core * RH, RH), RH)
    part, columns = g4.shape[1], g4.shape[2]
    at_x, at_y, at_s, at_d = (d + dx, z), (d + dy, z), (d + ds_, z), (d + dx + dy, z)
    pairs = DP // 2
    others = [lax.rem(d + 2 * j, DP) for j in range(1, pairs)]

    barrier = pltpu.get_barrier_semaphore()
    for k in range(Z - 1):
        pl.semaphore_signal(barrier, inc=1, device_id=(d, source(k)), device_id_type=MESH)
    for o in others:
        pl.semaphore_signal(barrier, inc=1, device_id=(o, z), device_id_type=MESH)
    pl.semaphore_signal(barrier, inc=1, device_id=at_s, device_id_type=MESH)

    code_loads = [
        pltpu.make_async_copy(codes_hbm.at[h * GROUP * blocks:(h + 1) * GROUP * blocks],
                              codes.at[h * GROUP * blocks:(h + 1) * GROUP * blocks], code_sem.at[h])
        for h in range(H)
    ]
    loads = [
        pltpu.make_async_copy(up_hbm, upf.at[z], load_sem.at[0]),
        pltpu.make_async_copy(grad_hbm, grad, load_sem.at[1]),
        pltpu.make_async_copy(acts_hbm, acts, load_sem.at[2]),
        pltpu.make_async_copy(scale_hbm, scale_ref, load_sem.at[3]),
        pltpu.make_async_copy(col_hbm, col_ref, load_sem.at[4]),
    ]
    down_loads = [
        pltpu.make_async_copy(down_hbm.at[:, q * tile:(q + 1) * tile], downf.at[z, q], down_sem.at[q])
        for q in range(GROUP)
    ]
    code_loads[0].start()
    loads[3].start()
    loads[4].start()
    loads[0].start()
    for c in down_loads:
        c.start()
    for c in code_loads[1:]:
        c.start()
    loads[1].start()
    loads[2].start()

    sends, conditions = [], {}

    def send(src, dst, sem, to):
        c = pltpu.make_async_remote_copy(src_ref=src, dst_ref=dst, send_sem=send_sem.at[len(sends)],
                                         recv_sem=sem, device_id=to, device_id_type=MESH)
        c.start()
        sends.append(c)

    def send_if(on, src, dst, sem, to):
        c = pltpu.make_async_remote_copy(src_ref=src, dst_ref=dst, send_sem=send_sem.at[len(sends)],
                                         recv_sem=sem, device_id=to, device_id_type=MESH)
        pl.when(on)(c.start)
        sends.append(c)
        conditions[len(sends) - 1] = on

    def arrived(ref, sem):
        pltpu.make_async_remote_copy(src_ref=ref, dst_ref=ref, send_sem=send_sem.at[0], recv_sem=sem,
                                     device_id=at_s, device_id_type=MESH).wait_recv()

    def send_w(s, h, q, to):
        send(weight.at[s, h, q], weight.at[s, h, q], w_sem.at[s, h, q], to)

    def send_w_if(on, s, h, q, to):
        send_if(on, weight.at[s, h, q], weight.at[s, h, q], w_sem.at[s, h, q], to)

    def wait_w(s, h, q):
        arrived(weight.at[s, h, q], w_sem.at[s, h, q])

    def share_w(s, h):
        piece = weight.at[s, h, pl.ds(here, side)]
        send(piece, piece, w_sem.at[s, h, here], at_s)

    def await_w(s, h):
        arrived(weight.at[s, h, pl.ds(there, side)], w_sem.at[s, h, there])

    def send_d(s, q, to):
        send(downf.at[s, q], downf.at[s, q], d_sem.at[s, q], to)

    def wait_d(s, q):
        arrived(downf.at[s, q], d_sem.at[s, q])

    def dequantize(h, q):
        for r in range(blocks):
            b = (h * GROUP + q) * blocks + r

            def columns(c, _, b=b, r=r):
                cols = pl.ds(pl.multiple_of(c * 256, 256), 256)
                words = codes[b, :, cols]
                absmax = (scale_ref[pl.ds(b, 1), cols].astype(jnp.float32) + 1.0) / 256.0 * col_ref[:, cols]
                for j in range(4):
                    stage[pl.ds(j, 16, stride=4), :] = levels_of(words, j)[:, :128] * absmax[:, :128]
                    stage[pl.ds(64 + j, 16, stride=4), :] = levels_of(words, j)[:, 128:] * absmax[:, 128:]
                weight[z, h, q, pl.ds(r * 64, 64), pl.ds(pl.multiple_of(c * 256, 128), 128)] = stage[0:64].astype(jnp.bfloat16)
                weight[z, h, q, pl.ds(r * 64, 64), pl.ds(pl.multiple_of(c * 256 + 128, 128), 128)] = stage[64:128].astype(jnp.bfloat16)
                return 0

            lax.fori_loop(0, width // 256, columns, 0)

    def tiles(s, h):
        def one(t, _):
            part = weight[s, h, pl.ds(H * t, H)].reshape(tile, width)
            tt = h * per + t
            acc = lax.dot_general(grad[...], part, NT, preferred_element_type=jnp.float32)
            acc += adapter_scale * jnp.dot(mix[...], downf[s, tt], preferred_element_type=jnp.float32)
            out_ref[:, pl.ds(pl.multiple_of((s * GROUP + tt) * tile, tile), tile)] = acc.astype(jnp.bfloat16)
            return 0

        lax.fori_loop(0, per, one, 0, unroll=2)

    px, py = p + 1 - 2 * xbit, p + 2 - 4 * ybit
    pd = px + py - p
    here, there = pl.multiple_of(side * core, side), pl.multiple_of(side * (1 - core), side)
    events = H * (Z - 1)

    def event(i):
        pair, r = i // (2 * H), i % (2 * H)
        both = i // H < 2 * near
        k = jnp.where(both, 2 * pair + r % 2, i // H)
        h = jnp.where(both, r // 2, i % H)
        paired = jnp.where(k % 2 == 0, z - (k // 2 + 1), z + (k // 2 + 1))
        rest = jnp.where(2 * z < Z - 1, z + (k - near + 1), z - (k - near + 1))
        return jnp.where(both, paired, rest), h

    def passes_on(s):
        return ((s < z) & (z < Z - 1)) | ((s > z) & (z > 0))

    def at_end(s):
        return (s == 0) | (s == Z - 1)

    def onward(s, on):
        return d, jnp.where(on, z + jnp.where(s < z, 1, -1), source(0))

    def pass_on(i):
        s, h = event(i)
        on = passes_on(s)
        pl.when(on)(lambda: wait_w(s, h, p))
        send_w_if(on, s, h, p, onward(s, on))

    def first(i):
        s, h = event(i)
        pl.when(jnp.logical_not(passes_on(s)))(lambda: wait_w(s, h, p))
        send_w(s, h, p, at_x)
        send_w(s, h, p, at_y)

    def second(i):
        s, h = event(i)
        even = h % 2 == 0
        wait_w(s, h, px)
        wait_w(s, h, py)
        send_w_if(jnp.logical_not(at_end(s)), s, h, jnp.where(even, px, py), (d + jnp.where(even, dy, dx), z))

    def third(i):
        s, h = event(i)
        pl.when(jnp.logical_not(at_end(s) & passes_on(s)))(lambda: wait_w(s, h, pd))
        share_w(s, h)

    def pass_far(i):
        s, h = event(i)
        on = at_end(s) & passes_on(s)
        pl.when(on)(lambda: wait_w(s, h, pd))
        send_w_if(on, s, h, pd, onward(s, on))

    def use(i):
        s, h = event(i)
        await_w(s, h)
        tiles(s, h)

    second_at, third_at, ahead_at, far_at = [], [], [], []
    tables = zip(*(spread(table, events) for table in (SECOND, THIRD, AHEAD, FAR)))
    for e, (lag2, lag3, lead, far) in enumerate(tables):
        second_at.append(max([e + lag2] + second_at[-1:]))
        third_at.append(max([e + lag3, second_at[e]] + third_at[-1:]))
        far_at.append(max([e + far] + far_at[-1:]))
        ahead_at.append(max([0, e - lead] + ahead_at[-1:]))

    def own(h):
        dequantize(h, px)
        dequantize(h, py)
        share_w(z, h)

    def own_use(h):
        await_w(z, h)
        tiles(z, h)

    def own_near(h):
        send_w_if(z < Z - 1, z, h, p, (d, jnp.where(z < Z - 1, z + 1, z - 1)))
        send_w_if(z > 0, z, h, p, (d, jnp.where(z > 0, z - 1, z + 1)))

    code_loads[0].wait()
    loads[3].wait()
    loads[4].wait()
    dequantize(0, p)
    pl.semaphore_wait(barrier, (Z - 1) + (pairs - 1) + 1)
    for c in down_loads:
        c.wait()
    for k in range(Z - 1):
        send_d(z, p, (d, source(k)))
    own_near(0)
    loads[0].wait()
    half = pl.ds(pl.multiple_of(core * RH, RH), RH)
    for k in range(Z - 1):
        send(upf.at[z, half], upf.at[z, half], u_sem.at[z, core], (d, source(k)))
    for h in range(1, H):
        code_loads[h].wait()
        dequantize(h, p)
        own_near(h)

    def own_far(h):
        dequantize(h, pd)
        send_w_if(at_end(z), z, h, pd, (d, jnp.where(z == 0, z + 1, z - 1)))

    def mixed():
        loads[1].wait()
        for k in range(Z - 1):
            piece = upf.at[source(k), half]
            arrived(piece, u_sem.at[source(k), core])
            send(piece, piece, u_sem.at[source(k), core], at_s)
        for k in range(Z - 1):
            arrived(upf.at[source(k), half], u_sem.at[source(k), 1 - core])
        total = jnp.zeros(mix.shape, jnp.float32)
        for s in range(Z):
            total += lax.dot_general(grad[:, s * up_width:(s + 1) * up_width], upf[s], NT,
                                     preferred_element_type=jnp.float32)
        mix[...] = total.astype(jnp.bfloat16)
        mix_t[...] = total.astype(jnp.bfloat16).astype(jnp.float32).T.astype(jnp.bfloat16)

    def down_first():
        for k in range(Z - 1):
            s = source(k)
            wait_d(s, p)
            for to in (at_x, at_y):
                send_d(s, p, to)

    def down_second():
        for k in range(Z - 1):
            s = source(k)
            for q in (px, py):
                wait_d(s, q)
            send_d(s, *((px, at_y) if k % 2 == 0 else (py, at_x)))

    def down_share():
        for k in range(Z - 1):
            s = source(k)
            wait_d(s, pd)
            piece = downf.at[s, pl.ds(here, side)]
            send(piece, piece, d_sem.at[s, here], at_s)

    def down_third():
        for k in range(Z - 1):
            arrived(downf.at[source(k), pl.ds(there, side)], d_sem.at[source(k), there])

    def products(k):
        s = z if k < 0 else source(k)
        if k < 0:
            loads[2].wait()

        def one(q, total):
            t = s * GROUP + q
            a = acts[:, pl.ds(pl.multiple_of(t * tile, tile), tile)]
            terms[s, :, pl.ds(pl.multiple_of(q * tile, tile), tile)] = jnp.dot(
                mix_t[...], a, preferred_element_type=jnp.float32)
            return total + lax.dot_general(a, downf[s, q], NT, preferred_element_type=jnp.float32)

        begin = jnp.zeros(mix.shape, jnp.float32) if k < 0 else low[...]
        low[...] = lax.fori_loop(0, GROUP, one, begin, unroll=2)

    def gradient_terms():
        low_t = low[...].astype(jnp.bfloat16).astype(jnp.float32).T.astype(jnp.bfloat16)
        for s in range(Z):
            terms[s, :, shard:shard + up_width] = jnp.dot(
                low_t, grad[:, s * up_width:(s + 1) * up_width], preferred_element_type=jnp.float32)
        if terms.shape[2] > shard + up_width:
            terms[:, :, shard + up_width:] = jnp.zeros((Z, R, terms.shape[2] - shard - up_width), jnp.float32)
        theirs = pl.multiple_of((1 - core) * RH, RH)
        for s in range(Z):
            g1s[s] = terms[s, pl.ds(theirs, RH), :].astype(jnp.bfloat16)
        send(g1s, g1r, g1_sem.at[0], at_s)

    def reduce_core():
        arrived(g1r, g1_sem.at[0])
        for s in range(Z):
            terms[s, mine, :] += g1r[s].astype(jnp.float32)

    edge = (z == 0) | (z == Z - 1)

    def chain(k, on):
        s = source(Z - 2 - k)
        down = s < z
        way = jnp.where(down, 0, 1)

        def add():
            terms[s, mine, :] += g2r[way, s].astype(jnp.float32)

        def pack():
            g2s[s] = terms[s, mine, :].astype(jnp.bfloat16)

        if on is not edge:
            pl.when(on)(lambda: arrived(g2r.at[way, s], g2_sem.at[way, s]))
            pl.when(on)(add)
        pl.when(on)(pack)
        send_if(on, g2s.at[s], g2r.at[way, s], g2_sem.at[way, s], (d, z + jnp.where(down, -1, 1)))

    def chain_ends():
        for k in range(Z - 1):
            chain(k, edge)

    slot = d // 2

    def home():
        for way, on in ((0, z < Z - 1), (1, z > 0)):
            def add(way=way):
                arrived(g2r.at[way, z], g2_sem.at[way, z])
                terms[z, mine, :] += g2r[way, z].astype(jnp.float32)

            pl.when(on)(add)
        total = terms[z, mine, :].astype(jnp.bfloat16)
        for j in range(pairs):
            g3s[j] = total[j % 2 * part:(j % 2 + 1) * part, j // 2 * columns:(j // 2 + 1) * columns]
        for o in others:
            send(g3s.at[o // 2], g3r.at[slot], g3_sem.at[slot], (o, z))

    def reduce_dp():
        total = g3s[slot].astype(jnp.float32)
        for o in others:
            arrived(g3r.at[o // 2], g3_sem.at[o // 2])
            total += g3r[o // 2].astype(jnp.float32)
        g4[slot] = total.astype(jnp.bfloat16)
        for o in others:
            send(g4.at[slot], g4.at[slot], g4_sem.at[slot], (o, z))

    def gather_dp():
        for o in others:
            arrived(g4.at[o // 2], g4_sem.at[o // 2])
        for j in range(pairs):
            fin[core, j % 2 * part:(j % 2 + 1) * part, j // 2 * columns:(j // 2 + 1) * columns] = factor * g4[j].astype(jnp.float32)
        send(fin.at[core], fin.at[core], fin_sem.at[0], at_s)

    def finish():
        arrived(fin.at[1 - core], fin_sem.at[0])
        for c in range(2):
            gdown_ref[c * RH:(c + 1) * RH, :] = fin[c, :, :shard]
            gup_ref[c * RH:(c + 1) * RH, :] = fin[c, :, shard:shard + up_width]

    for h in range(max(1, H - 2)):
        own_far(h)
    down_first()
    for h in range(max(1, H - 2), H):
        own_far(h)

    work = [[] for _ in range(GATHER + events)]
    work[DOWN].append(down_second)
    work[MIX].append(mixed)
    for k, i in enumerate(spread(PRODUCTS, Z)):
        if k == 1:
            work[i].extend([down_share, down_third])
        work[i].append(lambda k=k: products(k - 1))
    work[PRODUCTS[-1]].append(gradient_terms)
    for h, i in enumerate(spread(DEQUANT, H)):
        work[i].append(lambda h=h: own(h))
    for h, i in enumerate(spread(OWN, H)):
        work[i].append(lambda h=h: own_use(h))
    work[CORE].append(reduce_core)
    work[CORE].append(chain_ends)
    for k, i in enumerate(spread(CHAIN, Z - 1)):
        work[i].append(lambda k=k: chain(k, jnp.logical_not(edge)))
    work[HOME].append(home)
    work[SPREAD].append(reduce_dp)
    work[GATHER].append(gather_dp)
    work[GATHER + 1].append(finish)

    issued, drained = [], [0]

    def drain(upto):
        for j in range(drained[0], upto):
            if j in conditions:
                pl.when(conditions[j])(sends[j].wait_send)
            else:
                sends[j].wait_send()
        drained[0] = upto

    for i in range(len(work)):
        if i == 0:
            pass_on(0)
        if i < events:
            first(i)
        for e in range(1, events):
            if ahead_at[e] == i:
                pass_on(e)
        for e in range(events):
            if second_at[e] == i:
                second(e)
        for e in range(events):
            if far_at[e] == i:
                pass_far(e)
        for e in range(events):
            if third_at[e] == i:
                third(e)
        for e in range(events):
            if third_at[e] == i - 1:
                use(e)
        for step in work[i]:
            step()
        issued.append(len(sends))
        if i >= LATE:
            drain(issued[i - LATE])

    drain(len(sends))


def write_out(held, gdown_held, gup_held, out_hbm, gdown_hbm, gup_hbm, sem):
    rows = held.shape[0] // STRIPES
    copies = [
        pltpu.make_async_copy(held.at[i * rows:(i + 1) * rows], out_hbm.at[i * rows:(i + 1) * rows], sem.at[i])
        for i in range(STRIPES)
    ]
    copies += [
        pltpu.make_async_copy(gdown_held, gdown_hbm, sem.at[STRIPES]),
        pltpu.make_async_copy(gup_held, gup_hbm, sem.at[STRIPES + 1]),
    ]
    for c in copies:
        c.start()
    for c in copies:
        c.wait()


def solution(mesh):
    Z, DP = mesh.shape["fsdp"], mesh.shape["dp"]
    bf16, f32 = jnp.bfloat16, jnp.float32

    def local(acts, grad_out, codes, scale_codes, col_scale, down_adapter, up_adapter):
        tokens, D = acts.shape
        O = grad_out.shape[1]
        R, shard = down_adapter.shape
        up_width = up_adapter.shape[1]
        tile = shard // GROUP
        wide = shard + up_width
        RH = R // 2
        factor = adapter_scale * float(tokens * Z * DP) ** (-0.5)
        blocks = codes.shape[0]
        H = max(1, blocks // GROUP)
        pairs = DP // 2
        part = RH // 2
        columns = -(-wide // (pairs // 2 * 128)) * 128
        wide = columns * (pairs // 2)
        n_sends = 4 * H + (Z - 1) * (3 + 4 + 6 * H + 2) + 1 + 2 * (pairs - 1) + 1
        DMA = pltpu.SemaphoreType.DMA
        anywhere, vmem = pl.BlockSpec(memory_space=pl.ANY), pl.BlockSpec(memory_space=pltpu.VMEM)
        held = pl.pallas_call(
            functools.partial(kernel, Z, DP, H, factor),
            out_shape=(
                pltpu.VMEM((tokens, D), bf16),
                pltpu.VMEM((R, shard), f32),
                pltpu.VMEM((R, up_width), f32),
            ),
            in_specs=[anywhere] * 7,
            out_specs=(vmem, vmem, vmem),
            scratch_shapes=[
                pltpu.VMEM((tokens, D), bf16),
                pltpu.VMEM((tokens, O), bf16),
                pltpu.VMEM(codes.shape, jnp.int32),
                pltpu.VMEM(scale_codes.shape, jnp.int32),
                pltpu.VMEM((1, O), f32),
                pltpu.VMEM((Z, H, GROUP, tile // H, O), bf16),
                pltpu.VMEM((Z, GROUP, R, tile), bf16),
                pltpu.VMEM((Z, R, up_width), bf16),
                pltpu.VMEM((128, 128), f32),
                pltpu.VMEM((tokens, R), bf16),
                pltpu.VMEM((R, tokens), bf16),
                pltpu.VMEM((tokens, R), f32),
                pltpu.VMEM((Z, R, wide), f32),
                pltpu.VMEM((Z, RH, wide), bf16),
                pltpu.VMEM((Z, RH, wide), bf16),
                pltpu.VMEM((Z, RH, wide), bf16),
                pltpu.VMEM((2, Z, RH, wide), bf16),
                pltpu.VMEM((pairs, part, columns), bf16),
                pltpu.VMEM((pairs, part, columns), bf16),
                pltpu.VMEM((pairs, part, columns), bf16),
                pltpu.VMEM((2, RH, wide), f32),
                DMA((5,)), DMA((H,)), DMA((GROUP,)), DMA((n_sends,)),
                DMA((Z, H, GROUP)), DMA((Z, GROUP)), DMA((Z, 2)),
                DMA((1,)), DMA((2, Z)), DMA((pairs,)), DMA((pairs,)), DMA((1,)),
            ],
            compiler_params=pltpu.CompilerParams(
                collective_id=0, has_side_effects=True, vmem_limit_bytes=52 * 1024 * 1024
            ),
        )(acts, grad_out, codes, scale_codes, col_scale.reshape(1, -1), down_adapter, up_adapter)
        return pl.pallas_call(
            write_out,
            out_shape=(
                jax.ShapeDtypeStruct((tokens, D), bf16),
                jax.ShapeDtypeStruct((R, shard), f32),
                jax.ShapeDtypeStruct((R, up_width), f32),
            ),
            in_specs=[vmem] * 3,
            out_specs=(anywhere,) * 3,
            scratch_shapes=[DMA((STRIPES + 2,))],
            compiler_params=pltpu.CompilerParams(vmem_limit_bytes=1024 * 1024),
        )(*[pltpu.with_memory_space_constraint(x, pltpu.VMEM) for x in held])

    placed = (
        P(("dp", "fsdp"), None),
        P(("dp", "fsdp"), None),
        P("fsdp", None, None),
        P("fsdp", None),
        P(),
        P(None, "fsdp"),
        P(None, "fsdp"),
    )
    return jax.shard_map(
        local,
        mesh=mesh,
        in_specs=placed,
        out_specs=(P(("dp", "fsdp"), None), P(None, "fsdp"), P(None, "fsdp")),
        check_vma=False,
    )
```

```python
import functools

import jax
import jax.numpy as jnp
from jax import lax
from jax.experimental import pallas as pl
from jax.experimental.pallas import tpu as pltpu
from jax.sharding import PartitionSpec as P

MESH = pl.DeviceIdType.MESH
NT = (((1,), (1,)), ((), ()))
adapter_scale = 0.5
nf4_table = [
    -1.0,
    -0.6961928009986877,
    -0.5250730514526367,
    -0.39491748809814453,
    -0.28444138169288635,
    -0.18477343022823334,
    -0.09105003625154495,
    0.0,
    0.07958029955625534,
    0.16093020141124725,
    0.24611230194568634,
    0.33791524171829224,
    0.44070982933044434,
    0.5626170039176941,
    0.7229568362236023,
    1.0,
]
GROUP = 8
STRIPES = 16
LATE = 8
SECOND = (2, 2, 3, 3, 2, 3, 2, 3, 3, 6, 7, 7)
THIRD = (5, 4, 7, 6, 9, 8, 8, 9, 8, 8, 8, 7)
FAR = (3, 3, 4, 3, 4, 4, 4, 3, 2, 2, 1, 6)
AHEAD = (0, 1, 1, 1, 2, 2, 3, 3, 4, 4, 3, 2)
PRODUCTS = (1, 2, 3, 4)
DEQUANT = (3, 4, 5, 7)
OWN = (6, 6, 9, 13)
CHAIN = (6, 9, 9)
MIX, DOWN, CORE, HOME, SPREAD, GATHER = (0, 0, 5, 10, 16, 18)


def spread(table, n):
    return [table[i * len(table) // n] for i in range(n)]


def levels_of(words, nibble):
    rows = [jnp.float32(v) for v in nf4_table]
    for bit in range(4):
        on = (words & (1 << (4 * nibble + bit))) != 0
        rows = [jnp.where(on, rows[2 * i + 1], rows[2 * i]) for i in range(len(rows) // 2)]
    return rows[0]


def kernel(Z, DP, H, factor, acts_hbm, grad_hbm, codes_hbm, scale_hbm, col_hbm, down_hbm, up_hbm,
           out_ref, gdown_ref, gup_ref,
           acts, grad, codes, scale_ref, col_ref, weight, downf, upf, stage, mix, mix_t, low, terms,
           g1s, g1r, g2s, g2r, g3s, g3r, g4, fin,
           load_sem, code_sem, down_sem, send_sem, w_sem, d_sem, u_sem, g1_sem, g2_sem, g3_sem, g4_sem, fin_sem):
    d, z = lax.axis_index("dp"), lax.axis_index("fsdp")
    core = lax.rem(d, 2)
    side = GROUP // 2
    p = side * core + lax.rem(d // 2, side)
    xbit, ybit = lax.rem(d // 2, 2), lax.rem(d // 4, 2)
    dx, dy, ds_ = 2 - 4 * xbit, 4 - 8 * ybit, 1 - 2 * core
    rows, width = weight.shape[3], weight.shape[4]
    tile = H * rows
    per = GROUP // H
    shard = GROUP * tile
    R = mix.shape[1]
    RH = R // 2
    up_width = upf.shape[2]
    blocks = rows // 64
    near = jnp.minimum(z, Z - 1 - z)

    def source(k):
        paired = jnp.where(k % 2 == 0, z - (k // 2 + 1), z + (k // 2 + 1))
        rest = jnp.where(2 * z < Z - 1, z + (k - near + 1), z - (k - near + 1))
        return jnp.where(k < 2 * near, paired, rest)

    mine = pl.ds(pl.multiple_of(core * RH, RH), RH)
    part, columns = g4.shape[1], g4.shape[2]
    at_x, at_y, at_s, at_d = (d + dx, z), (d + dy, z), (d + ds_, z), (d + dx + dy, z)
    pairs = DP // 2
    others = [lax.rem(d + 2 * j, DP) for j in range(1, pairs)]

    barrier = pltpu.get_barrier_semaphore()
    for k in range(Z - 1):
        pl.semaphore_signal(barrier, inc=1, device_id=(d, source(k)), device_id_type=MESH)
    for o in others:
        pl.semaphore_signal(barrier, inc=1, device_id=(o, z), device_id_type=MESH)
    pl.semaphore_signal(barrier, inc=1, device_id=at_s, device_id_type=MESH)

    code_loads = [
        pltpu.make_async_copy(codes_hbm.at[h * GROUP * blocks:(h + 1) * GROUP * blocks],
                              codes.at[h * GROUP * blocks:(h + 1) * GROUP * blocks], code_sem.at[h])
        for h in range(H)
    ]
    loads = [
        pltpu.make_async_copy(up_hbm, upf.at[z], load_sem.at[0]),
        pltpu.make_async_copy(grad_hbm, grad, load_sem.at[1]),
        pltpu.make_async_copy(acts_hbm, acts, load_sem.at[2]),
        pltpu.make_async_copy(scale_hbm, scale_ref, load_sem.at[3]),
        pltpu.make_async_copy(col_hbm, col_ref, load_sem.at[4]),
    ]
    down_loads = [
        pltpu.make_async_copy(down_hbm.at[:, q * tile:(q + 1) * tile], downf.at[z, q], down_sem.at[q])
        for q in range(GROUP)
    ]
    code_loads[0].start()
    loads[3].start()
    loads[4].start()
    loads[0].start()
    for c in down_loads:
        c.start()
    for c in code_loads[1:]:
        c.start()
    loads[1].start()
    loads[2].start()

    sends, conditions = [], {}

    def send(src, dst, sem, to):
        c = pltpu.make_async_remote_copy(src_ref=src, dst_ref=dst, send_sem=send_sem.at[len(sends)],
                                         recv_sem=sem, device_id=to, device_id_type=MESH)
        c.start()
        sends.append(c)

    def send_if(on, src, dst, sem, to):
        c = pltpu.make_async_remote_copy(src_ref=src, dst_ref=dst, send_sem=send_sem.at[len(sends)],
                                         recv_sem=sem, device_id=to, device_id_type=MESH)
        pl.when(on)(c.start)
        sends.append(c)
        conditions[len(sends) - 1] = on

    def arrived(ref, sem):
        pltpu.make_async_remote_copy(src_ref=ref, dst_ref=ref, send_sem=send_sem.at[0], recv_sem=sem,
                                     device_id=at_s, device_id_type=MESH).wait_recv()

    def send_w(s, h, q, to):
        send(weight.at[s, h, q], weight.at[s, h, q], w_sem.at[s, h, q], to)

    def send_w_if(on, s, h, q, to):
        send_if(on, weight.at[s, h, q], weight.at[s, h, q], w_sem.at[s, h, q], to)

    def wait_w(s, h, q):
        arrived(weight.at[s, h, q], w_sem.at[s, h, q])

    def share_w(s, h):
        piece = weight.at[s, h, pl.ds(here, side)]
        send(piece, piece, w_sem.at[s, h, here], at_s)

    def await_w(s, h):
        arrived(weight.at[s, h, pl.ds(there, side)], w_sem.at[s, h, there])

    def send_d(s, q, to):
        send(downf.at[s, q], downf.at[s, q], d_sem.at[s, q], to)

    def wait_d(s, q):
        arrived(downf.at[s, q], d_sem.at[s, q])

    def dequantize(h, q):
        for r in range(blocks):
            b = (h * GROUP + q) * blocks + r

            def columns(c, _, b=b, r=r):
                cols = pl.ds(pl.multiple_of(c * 256, 256), 256)
                words = codes[b, :, cols]
                absmax = (scale_ref[pl.ds(b, 1), cols].astype(jnp.float32) + 1.0) / 256.0 * col_ref[:, cols]
                for j in range(4):
                    stage[pl.ds(j, 16, stride=4), :] = levels_of(words, j)[:, :128] * absmax[:, :128]
                    stage[pl.ds(64 + j, 16, stride=4), :] = levels_of(words, j)[:, 128:] * absmax[:, 128:]
                weight[z, h, q, pl.ds(r * 64, 64), pl.ds(pl.multiple_of(c * 256, 128), 128)] = stage[0:64].astype(jnp.bfloat16)
                weight[z, h, q, pl.ds(r * 64, 64), pl.ds(pl.multiple_of(c * 256 + 128, 128), 128)] = stage[64:128].astype(jnp.bfloat16)
                return 0

            lax.fori_loop(0, width // 256, columns, 0)

    def tiles(s, h):
        def one(t, _):
            part = weight[s, h, pl.ds(H * t, H)].reshape(tile, width)
            tt = h * per + t
            acc = lax.dot_general(grad[...], part, NT, preferred_element_type=jnp.float32)
            acc += adapter_scale * jnp.dot(mix[...], downf[s, tt], preferred_element_type=jnp.float32)
            out_ref[:, pl.ds(pl.multiple_of((s * GROUP + tt) * tile, tile), tile)] = acc.astype(jnp.bfloat16)
            return 0

        lax.fori_loop(0, per, one, 0, unroll=2)

    px, py = p + 1 - 2 * xbit, p + 2 - 4 * ybit
    pd = px + py - p
    here, there = pl.multiple_of(side * core, side), pl.multiple_of(side * (1 - core), side)
    events = H * (Z - 1)

    def event(i):
        pair, r = i // (2 * H), i % (2 * H)
        both = i // H < 2 * near
        k = jnp.where(both, 2 * pair + r % 2, i // H)
        h = jnp.where(both, r // 2, i % H)
        paired = jnp.where(k % 2 == 0, z - (k // 2 + 1), z + (k // 2 + 1))
        rest = jnp.where(2 * z < Z - 1, z + (k - near + 1), z - (k - near + 1))
        return jnp.where(both, paired, rest), h

    def passes_on(s):
        return ((s < z) & (z < Z - 1)) | ((s > z) & (z > 0))

    def at_end(s):
        return (s == 0) | (s == Z - 1)

    def onward(s, on):
        return d, jnp.where(on, z + jnp.where(s < z, 1, -1), source(0))

    def pass_on(i):
        s, h = event(i)
        on = passes_on(s)
        pl.when(on)(lambda: wait_w(s, h, p))
        send_w_if(on, s, h, p, onward(s, on))

    def first(i):
        s, h = event(i)
        pl.when(jnp.logical_not(passes_on(s)))(lambda: wait_w(s, h, p))
        send_w(s, h, p, at_x)
        send_w(s, h, p, at_y)

    def second(i):
        s, h = event(i)
        even = h % 2 == 0
        wait_w(s, h, px)
        wait_w(s, h, py)
        send_w_if(jnp.logical_not(at_end(s)), s, h, jnp.where(even, px, py), (d + jnp.where(even, dy, dx), z))

    def third(i):
        s, h = event(i)
        pl.when(jnp.logical_not(at_end(s) & passes_on(s)))(lambda: wait_w(s, h, pd))
        share_w(s, h)

    def pass_far(i):
        s, h = event(i)
        on = at_end(s) & passes_on(s)
        pl.when(on)(lambda: wait_w(s, h, pd))
        send_w_if(on, s, h, pd, onward(s, on))

    def use(i):
        s, h = event(i)
        await_w(s, h)
        tiles(s, h)

    second_at, third_at, ahead_at, far_at = [], [], [], []
    tables = zip(*(spread(table, events) for table in (SECOND, THIRD, AHEAD, FAR)))
    for e, (lag2, lag3, lead, far) in enumerate(tables):
        second_at.append(max([e + lag2] + second_at[-1:]))
        third_at.append(max([e + lag3, second_at[e]] + third_at[-1:]))
        far_at.append(max([e + far] + far_at[-1:]))
        ahead_at.append(max([0, e - lead] + ahead_at[-1:]))

    def own(h):
        dequantize(h, px)
        dequantize(h, py)
        share_w(z, h)

    def own_use(h):
        await_w(z, h)
        tiles(z, h)

    def own_near(h):
        send_w_if(z < Z - 1, z, h, p, (d, jnp.where(z < Z - 1, z + 1, z - 1)))
        send_w_if(z > 0, z, h, p, (d, jnp.where(z > 0, z - 1, z + 1)))

    code_loads[0].wait()
    loads[3].wait()
    loads[4].wait()
    dequantize(0, p)
    pl.semaphore_wait(barrier, (Z - 1) + (pairs - 1) + 1)
    for c in down_loads:
        c.wait()
    for k in range(Z - 1):
        send_d(z, p, (d, source(k)))
    own_near(0)
    loads[0].wait()
    half = pl.ds(pl.multiple_of(core * RH, RH), RH)
    for k in range(Z - 1):
        send(upf.at[z, half], upf.at[z, half], u_sem.at[z, core], (d, source(k)))
    for h in range(1, H):
        code_loads[h].wait()
        dequantize(h, p)
        own_near(h)

    def own_far(h):
        dequantize(h, pd)
        send_w_if(at_end(z), z, h, pd, (d, jnp.where(z == 0, z + 1, z - 1)))

    def mixed():
        loads[1].wait()
        for k in range(Z - 1):
            piece = upf.at[source(k), half]
            arrived(piece, u_sem.at[source(k), core])
            send(piece, piece, u_sem.at[source(k), core], at_s)
        for k in range(Z - 1):
            arrived(upf.at[source(k), half], u_sem.at[source(k), 1 - core])
        total = jnp.zeros(mix.shape, jnp.float32)
        for s in range(Z):
            total += lax.dot_general(grad[:, s * up_width:(s + 1) * up_width], upf[s], NT,
                                     preferred_element_type=jnp.float32)
        mix[...] = total.astype(jnp.bfloat16)
        mix_t[...] = total.astype(jnp.bfloat16).astype(jnp.float32).T.astype(jnp.bfloat16)

    def down_first():
        for k in range(Z - 1):
            s = source(k)
            wait_d(s, p)
            for to in (at_x, at_y):
                send_d(s, p, to)

    def down_second():
        for k in range(Z - 1):
            s = source(k)
            for q in (px, py):
                wait_d(s, q)
            send_d(s, *((px, at_y) if k % 2 == 0 else (py, at_x)))

    def down_share():
        for k in range(Z - 1):
            s = source(k)
            wait_d(s, pd)
            piece = downf.at[s, pl.ds(here, side)]
            send(piece, piece, d_sem.at[s, here], at_s)

    def down_third():
        for k in range(Z - 1):
            arrived(downf.at[source(k), pl.ds(there, side)], d_sem.at[source(k), there])

    def products(k):
        s = z if k < 0 else source(k)
        if k < 0:
            loads[2].wait()

        def one(q, total):
            t = s * GROUP + q
            a = acts[:, pl.ds(pl.multiple_of(t * tile, tile), tile)]
            terms[s, :, pl.ds(pl.multiple_of(q * tile, tile), tile)] = jnp.dot(
                mix_t[...], a, preferred_element_type=jnp.float32)
            return total + lax.dot_general(a, downf[s, q], NT, preferred_element_type=jnp.float32)

        begin = jnp.zeros(mix.shape, jnp.float32) if k < 0 else low[...]
        low[...] = lax.fori_loop(0, GROUP, one, begin, unroll=2)

    def gradient_terms():
        low_t = low[...].astype(jnp.bfloat16).astype(jnp.float32).T.astype(jnp.bfloat16)
        for s in range(Z):
            terms[s, :, shard:shard + up_width] = jnp.dot(
                low_t, grad[:, s * up_width:(s + 1) * up_width], preferred_element_type=jnp.float32)
        if terms.shape[2] > shard + up_width:
            terms[:, :, shard + up_width:] = jnp.zeros((Z, R, terms.shape[2] - shard - up_width), jnp.float32)
        theirs = pl.multiple_of((1 - core) * RH, RH)
        for s in range(Z):
            g1s[s] = terms[s, pl.ds(theirs, RH), :].astype(jnp.bfloat16)
        send(g1s, g1r, g1_sem.at[0], at_s)

    def reduce_core():
        arrived(g1r, g1_sem.at[0])
        for s in range(Z):
            terms[s, mine, :] += g1r[s].astype(jnp.float32)

    edge = (z == 0) | (z == Z - 1)

    def chain(k, on):
        s = source(Z - 2 - k)
        down = s < z
        way = jnp.where(down, 0, 1)

        def add():
            terms[s, mine, :] += g2r[way, s].astype(jnp.float32)

        def pack():
            g2s[s] = terms[s, mine, :].astype(jnp.bfloat16)

        if on is not edge:
            pl.when(on)(lambda: arrived(g2r.at[way, s], g2_sem.at[way, s]))
            pl.when(on)(add)
        pl.when(on)(pack)
        send_if(on, g2s.at[s], g2r.at[way, s], g2_sem.at[way, s], (d, z + jnp.where(down, -1, 1)))

    def chain_ends():
        for k in range(Z - 1):
            chain(k, edge)

    slot = d // 2

    def home():
        for way, on in ((0, z < Z - 1), (1, z > 0)):
            def add(way=way):
                arrived(g2r.at[way, z], g2_sem.at[way, z])
                terms[z, mine, :] += g2r[way, z].astype(jnp.float32)

            pl.when(on)(add)
        total = terms[z, mine, :].astype(jnp.bfloat16)
        for j in range(pairs):
            g3s[j] = total[j % 2 * part:(j % 2 + 1) * part, j // 2 * columns:(j // 2 + 1) * columns]
        for o in others:
            send(g3s.at[o // 2], g3r.at[slot], g3_sem.at[slot], (o, z))

    def reduce_dp():
        total = g3s[slot].astype(jnp.float32)
        for o in others:
            arrived(g3r.at[o // 2], g3_sem.at[o // 2])
            total += g3r[o // 2].astype(jnp.float32)
        g4[slot] = total.astype(jnp.bfloat16)
        for o in others:
            send(g4.at[slot], g4.at[slot], g4_sem.at[slot], (o, z))

    def gather_dp():
        for o in others:
            arrived(g4.at[o // 2], g4_sem.at[o // 2])
        for j in range(pairs):
            fin[core, j % 2 * part:(j % 2 + 1) * part, j // 2 * columns:(j // 2 + 1) * columns] = factor * g4[j].astype(jnp.float32)
        send(fin.at[core], fin.at[core], fin_sem.at[0], at_s)

    def finish():
        arrived(fin.at[1 - core], fin_sem.at[0])
        for c in range(2):
            gdown_ref[c * RH:(c + 1) * RH, :] = fin[c, :, :shard]
            gup_ref[c * RH:(c + 1) * RH, :] = fin[c, :, shard:shard + up_width]

    down_first()
    for h in range(H):
        own_far(h)

    work = [[] for _ in range(GATHER + events)]
    work[DOWN].append(down_second)
    work[MIX].append(mixed)
    for k, i in enumerate(spread(PRODUCTS, Z)):
        if k == 1:
            work[i].extend([down_share, down_third])
        work[i].append(lambda k=k: products(k - 1))
    work[PRODUCTS[-1]].append(gradient_terms)
    for h, i in enumerate(spread(DEQUANT, H)):
        work[i].append(lambda h=h: own(h))
    for h, i in enumerate(spread(OWN, H)):
        work[i].append(lambda h=h: own_use(h))
    work[CORE].append(reduce_core)
    work[CORE].append(chain_ends)
    for k, i in enumerate(spread(CHAIN, Z - 1)):
        work[i].append(lambda k=k: chain(k, jnp.logical_not(edge)))
    work[HOME].append(home)
    work[SPREAD].append(reduce_dp)
    work[GATHER].append(gather_dp)
    work[GATHER + 1].append(finish)

    issued, drained = [], [0]

    def drain(upto):
        for j in range(drained[0], upto):
            if j in conditions:
                pl.when(conditions[j])(sends[j].wait_send)
            else:
                sends[j].wait_send()
        drained[0] = upto

    for i in range(len(work)):
        if i == 0:
            pass_on(0)
        if i < events:
            first(i)
        for e in range(1, events):
            if ahead_at[e] == i:
                pass_on(e)
        for e in range(events):
            if second_at[e] == i:
                second(e)
        for e in range(events):
            if far_at[e] == i:
                pass_far(e)
        for e in range(events):
            if third_at[e] == i:
                third(e)
        for e in range(events):
            if third_at[e] == i - 1:
                use(e)
        for step in work[i]:
            step()
        issued.append(len(sends))
        if i >= LATE:
            drain(issued[i - LATE])

    drain(len(sends))


def write_out(held, gdown_held, gup_held, out_hbm, gdown_hbm, gup_hbm, sem):
    rows = held.shape[0] // STRIPES
    copies = [
        pltpu.make_async_copy(held.at[i * rows:(i + 1) * rows], out_hbm.at[i * rows:(i + 1) * rows], sem.at[i])
        for i in range(STRIPES)
    ]
    copies += [
        pltpu.make_async_copy(gdown_held, gdown_hbm, sem.at[STRIPES]),
        pltpu.make_async_copy(gup_held, gup_hbm, sem.at[STRIPES + 1]),
    ]
    for c in copies:
        c.start()
    for c in copies:
        c.wait()


def solution(mesh):
    Z, DP = mesh.shape["fsdp"], mesh.shape["dp"]
    bf16, f32 = jnp.bfloat16, jnp.float32

    def local(acts, grad_out, codes, scale_codes, col_scale, down_adapter, up_adapter):
        tokens, D = acts.shape
        O = grad_out.shape[1]
        R, shard = down_adapter.shape
        up_width = up_adapter.shape[1]
        tile = shard // GROUP
        wide = shard + up_width
        RH = R // 2
        factor = adapter_scale * float(tokens * Z * DP) ** (-0.5)
        blocks = codes.shape[0]
        H = max(1, blocks // GROUP)
        pairs = DP // 2
        part = RH // 2
        columns = -(-wide // (pairs // 2 * 128)) * 128
        wide = columns * (pairs // 2)
        n_sends = 4 * H + (Z - 1) * (3 + 4 + 6 * H + 2) + 1 + 2 * (pairs - 1) + 1
        DMA = pltpu.SemaphoreType.DMA
        anywhere, vmem = pl.BlockSpec(memory_space=pl.ANY), pl.BlockSpec(memory_space=pltpu.VMEM)
        held = pl.pallas_call(
            functools.partial(kernel, Z, DP, H, factor),
            out_shape=(
                pltpu.VMEM((tokens, D), bf16),
                pltpu.VMEM((R, shard), f32),
                pltpu.VMEM((R, up_width), f32),
            ),
            in_specs=[anywhere] * 7,
            out_specs=(vmem, vmem, vmem),
            scratch_shapes=[
                pltpu.VMEM((tokens, D), bf16),
                pltpu.VMEM((tokens, O), bf16),
                pltpu.VMEM(codes.shape, jnp.int32),
                pltpu.VMEM(scale_codes.shape, jnp.int32),
                pltpu.VMEM((1, O), f32),
                pltpu.VMEM((Z, H, GROUP, tile // H, O), bf16),
                pltpu.VMEM((Z, GROUP, R, tile), bf16),
                pltpu.VMEM((Z, R, up_width), bf16),
                pltpu.VMEM((128, 128), f32),
                pltpu.VMEM((tokens, R), bf16),
                pltpu.VMEM((R, tokens), bf16),
                pltpu.VMEM((tokens, R), f32),
                pltpu.VMEM((Z, R, wide), f32),
                pltpu.VMEM((Z, RH, wide), bf16),
                pltpu.VMEM((Z, RH, wide), bf16),
                pltpu.VMEM((Z, RH, wide), bf16),
                pltpu.VMEM((2, Z, RH, wide), bf16),
                pltpu.VMEM((pairs, part, columns), bf16),
                pltpu.VMEM((pairs, part, columns), bf16),
                pltpu.VMEM((pairs, part, columns), bf16),
                pltpu.VMEM((2, RH, wide), f32),
                DMA((5,)), DMA((H,)), DMA((GROUP,)), DMA((n_sends,)),
                DMA((Z, H, GROUP)), DMA((Z, GROUP)), DMA((Z, 2)),
                DMA((1,)), DMA((2, Z)), DMA((pairs,)), DMA((pairs,)), DMA((1,)),
            ],
            compiler_params=pltpu.CompilerParams(
                collective_id=0, has_side_effects=True, vmem_limit_bytes=52 * 1024 * 1024
            ),
        )(acts, grad_out, codes, scale_codes, col_scale.reshape(1, -1), down_adapter, up_adapter)
        return pl.pallas_call(
            write_out,
            out_shape=(
                jax.ShapeDtypeStruct((tokens, D), bf16),
                jax.ShapeDtypeStruct((R, shard), f32),
                jax.ShapeDtypeStruct((R, up_width), f32),
            ),
            in_specs=[vmem] * 3,
            out_specs=(anywhere,) * 3,
            scratch_shapes=[DMA((STRIPES + 2,))],
            compiler_params=pltpu.CompilerParams(vmem_limit_bytes=1024 * 1024),
        )(*[pltpu.with_memory_space_constraint(x, pltpu.VMEM) for x in held])

    placed = (
        P(("dp", "fsdp"), None),
        P(("dp", "fsdp"), None),
        P("fsdp", None, None),
        P("fsdp", None),
        P(),
        P(None, "fsdp"),
        P(None, "fsdp"),
    )
    return jax.shard_map(
        local,
        mesh=mesh,
        in_specs=placed,
        out_specs=(P(("dp", "fsdp"), None), P(None, "fsdp"), P(None, "fsdp")),
        check_vma=False,
    )
```
